128 devices in a mesh: dp: 32 (over z, x, core), mp: 4 (over y).
Axes of the slice: x: 4, y: 4, z: 4, core: 2. Of those that a mesh axis runs over, the one named last changes fastest.
Arguments:
- acts: bfloat16 [24576, 4, 1984], P('dp', 'mp'), may hold values from -6 to 6
- grads: bfloat16 [24576, 4, 1984], P('dp', 'mp'), may hold values from -0.21875 to 0.21875
- error: bfloat16 [32, 4, 1984, 1984], P('dp', 'mp'), may hold values from -4 to 4
- momentum: float32 [4, 1984, 1984], P('mp', 'dp'), may hold values from -4 to 4
- q_start: float32 [4, 1984, 128], P('mp'), may hold values from -0.125 to 0.125
Outputs:
- error_next: bfloat16 [32, 4, 1984, 1984], P('dp', 'mp')
- momentum_next: float32 [4, 1984, 1984], P('mp', 'dp')
- q_next: float32 [4, 1984, 128], P('mp')
The draws below stay inside these ranges and needn't reach their ends.
All inputs are finite; a program needn't handle non-finite values.
Results may differ from the reference program's by a relative error of at most 0.001.
Values sent between devices are 32-bit elements; how exact they have to be, the bound alone decides.
A program may use at most 128 MiB of HBM per device.

```python
import jax
import jax.numpy as jnp
from jax import lax

D = 3968
RANK = 128
TOK_DEV = 768
TILE = 1984
TOKENS = 24576
N_DP = 32
N_MP = 4


def levels(stream_key, extent, cuts, smallest, high):
    loudness, own = 1.0, jax.random.fold_in(stream_key, 6)
    for dim, blocks in cuts:
        steps = jnp.exp(jax.random.uniform(jax.random.fold_in(own, dim), (blocks,), jnp.float32, smallest / len(cuts), high / len(cuts)))
        loudness = loudness * jnp.repeat(steps, extent[dim] // blocks).reshape([-1 if axis == dim else 1 for axis in range(len(extent))])
    return loudness


def noise(own_key, dims, deviation, reach, cuts=(), dtype=jnp.bfloat16):
    drawn = jax.random.normal(own_key, dims, jnp.float32) * deviation
    if len(cuts) > 0:
        drawn = levels(own_key, dims, cuts, -0.22, 0.18) * drawn
    return jnp.clip(drawn, min=-reach, max=reach).astype(dtype)


def setup_inputs(seed: int = 0) -> dict:
    key_list = jax.random.split(jax.random.key(seed), 6)
    acts = noise(key_list[0], (TOKENS, N_MP, TILE), 1.0, 6.0, ((0, 32), (1, 4)))
    grads = noise(key_list[1], (TOKENS, N_MP, TILE), TOK_DEV ** -0.5, 0.21875, ((0, 32), (1, 4)))
    error = noise(key_list[2], (N_DP, N_MP, TILE, TILE), 0.5, 4.0, ((0, 32), (1, 4)))
    momentum = noise(key_list[3], (N_MP, TILE, TILE), 0.5, 4.0, ((0, 4), (1, 32)), jnp.float32)
    q_start = noise(key_list[4], (N_MP, TILE, RANK), TILE ** -0.5, 0.125, ((0, 4),), jnp.float32)
    return {"acts": acts, "grads": grads, "error": error, "momentum": momentum, "q_start": q_start}


PRECISE = lax.Precision.HIGHEST

def merged_of(inputs, upstream, stored):
    local_grad = lax.dot_general(inputs.astype(jnp.float32), upstream.astype(jnp.float32), (((0,), (0,)), ((), ())), preferred_element_type=jnp.float32)
    return local_grad + stored.astype(jnp.float32)

def tile_step(pieces):
    acts_tile, grads_tile, error_tile, warm_start = pieces

    def add_left(carry, item):
        merged = merged_of(item[0], item[1], item[2])
        return (carry + jnp.dot(merged, warm_start, precision=PRECISE), None)
    left_full, unused = lax.scan(add_left, jnp.zeros((TILE, RANK), jnp.float32), (acts_tile, grads_tile, error_tile))
    gram_matrix = jnp.dot(left_full.T, left_full, precision=PRECISE)
    cholesky_low = jnp.linalg.cholesky(gram_matrix)
    ortho_basis = lax.linalg.triangular_solve(cholesky_low, left_full, left_side=False, lower=True, transpose_a=True)

    def add_right(carry, item):
        merged = merged_of(item[0], item[1], item[2])
        part_right = lax.dot_general(merged, ortho_basis, (((0,), (0,)), ((), ())), precision=PRECISE)
        return (carry + part_right, None)
    right_full, unused = lax.scan(add_right, jnp.zeros((TILE, RANK), jnp.float32), (acts_tile, grads_tile, error_tile))
    q_tile = right_full / N_DP
    decoded = jnp.dot(ortho_basis, q_tile.T, precision=PRECISE)

    def new_error(item):
        return (merged_of(item[0], item[1], item[2]) - decoded).astype(jnp.bfloat16)
    errors_out = lax.map(new_error, (acts_tile, grads_tile, error_tile))
    return (ortho_basis, q_tile, errors_out)

def reference(acts, grads, error, momentum, q_start):
    acts_tiles = acts.reshape(N_DP, TOK_DEV, N_MP, TILE).transpose(2, 0, 1, 3)
    grads_tiles = grads.reshape(N_DP, TOK_DEV, N_MP, TILE).transpose(2, 0, 1, 3)
    error_tiles = error.transpose(1, 0, 2, 3)
    ortho_all, q_next, errors_all = lax.map(tile_step, (acts_tiles, grads_tiles, error_tiles, q_start))
    norm_total = jnp.sum(q_next * q_next)
    rms_value = jnp.sqrt(norm_total / (D * D))
    decoded_all = jnp.einsum('tir,tjr->tij', ortho_all, q_next, precision=PRECISE)
    momentum_next = 0.9 * momentum + 0.1 * decoded_all / (rms_value + 1e-06)
    return (errors_all.transpose(1, 0, 2, 3), momentum_next, q_next)
```

```python
import jax
import jax.numpy as jnp
from jax import lax
from jax.experimental import pallas as pl
from jax.experimental.pallas import tpu as pltpu
from jax.sharding import Mesh
from jax.sharding import PartitionSpec as P

D = 3968
DP = ("dp_0", "dp_1", "dp_2")
MESH = pl.DeviceIdType.MESH
TILE = 1984
PAD = 2048
RANK = 128
TOK = 768
CH = 128
NCH = 16
PIECE = 256
F32 = jnp.float32
BF16 = jnp.bfloat16
PRECISE = lax.Precision.HIGHEST
ORDER = (2, 1, 3, 0)
N_MSG = 27


def mm(a, b):
    return jnp.dot(a, b, preferred_element_type=F32)


def mm_t(a, b):
    return lax.dot_general(a, b, (((1,), (1,)), ((), ())), preferred_element_type=F32)


def split(v):
    hi = v.astype(BF16)
    return hi, (v - hi.astype(F32)).astype(BF16)


class Sum:
    def __init__(self, pos, bufs, sems, base):
        self.z, self.x, self.c, self.y = pos
        self.xs, self.sib, self.buf, self.relay, self.slots, self.out = bufs
        self.send, self.recv = sems
        self.base = base
        self.started = []
        z, x, c = self.z, self.x, self.c
        self.p = (1 - c) * x + c * z
        self.q = (1 - c) * z + c * x
        self.other_p = c * x + (1 - c) * z

    def along_first(self, d):
        return (lax.rem(self.z + self.c * d, 4), lax.rem(self.x + (1 - self.c) * d, 4), self.c, self.y)

    def along_second(self, d):
        return (lax.rem(self.z + (1 - self.c) * d, 4), lax.rem(self.x + self.c * d, 4), self.c, self.y)

    def sibling(self):
        return (self.z, self.x, 1 - self.c, self.y)

    def copy(self, i, src, dst, to):
        made = pltpu.make_async_remote_copy(
            src_ref=src,
            dst_ref=dst,
            send_sem=self.send.at[self.base + i],
            recv_sem=self.recv.at[self.base + i],
            device_id=to,
            device_id_type=MESH,
        )
        made.start()
        self.started.append(made)
        return made

    def sibling_piece(self, n):
        pos = lax.rem(self.other_p + ORDER[n], 4)
        return 4 * (1 - self.c) + pos

    def own_piece(self, n):
        return 4 * self.c + lax.rem(self.p + ORDER[n], 4)

    def send_sibling(self, n):
        i = 2 * self.sibling_piece(n)
        self.from_sibling = getattr(self, "from_sibling", {})
        self.from_sibling[n] = self.copy(n, self.xs.at[pl.ds(i, 2)], self.sib.at[n], self.sibling())

    def own_ready(self, n):
        i = 2 * self.own_piece(n)
        self.from_sibling[n].wait_recv()
        for s in range(2):
            self.xs[i + s] = self.xs[i + s] + self.sib[n, s]
        right, left = self.along_first(1), self.along_first(3)
        if n == 0:
            self.a_r = self.copy(4, self.xs.at[i], self.buf.at[0], right)
            self.a_l = self.copy(5, self.xs.at[i + 1], self.buf.at[1], left)
        elif n == 1:
            self.d_r = self.copy(6, self.xs.at[i + 1], self.buf.at[2], right)
        elif n == 2:
            self.d_l = self.copy(7, self.xs.at[i], self.buf.at[3], left)

    def pass_on(self):
        right, left = self.along_first(1), self.along_first(3)
        self.a_r.wait_recv()
        self.relay[0] = self.xs[2 * self.own_piece(1)] + self.buf[0]
        self.b_r = self.copy(8, self.relay.at[0], self.buf.at[4], right)
        self.a_l.wait_recv()
        self.relay[1] = self.xs[2 * self.own_piece(2) + 1] + self.buf[1]
        self.b_l = self.copy(9, self.relay.at[1], self.buf.at[5], left)

    def finish_first(self):
        i = 2 * self.own_piece(3)
        self.b_r.wait_recv()
        self.d_l.wait_recv()
        self.slots[2 * self.q] = self.xs[i] + self.buf[4] + self.buf[3]
        self.d_r.wait_recv()
        self.b_l.wait_recv()
        self.slots[2 * self.q + 1] = self.xs[i + 1] + self.buf[2] + self.buf[5]

    def spread(self, base, ref, at, right, left):
        own = ref.at[at], ref.at[at + 1]
        r0 = self.copy(base, own[0], own[0], right)
        l1 = self.copy(base + 1, own[1], own[1], left)
        r1 = self.copy(base + 2, own[1], own[1], right)
        l0 = self.copy(base + 3, own[0], own[0], left)
        return r0, l1, r1, l0

    def spread_on(self, base, ref, sent, from_left, from_right, right, left):
        r0, l1, _, _ = sent
        r0.wait_recv()
        f_r = self.copy(base + 4, ref.at[from_left], ref.at[from_left], right)
        l1.wait_recv()
        f_l = self.copy(base + 5, ref.at[from_right + 1], ref.at[from_right + 1], left)
        return f_r, f_l

    def second_start(self):
        self.s_sent = self.spread(10, self.slots, 2 * self.q, self.along_second(1), self.along_second(3))

    def second_pass_on(self):
        lf, rt = 2 * lax.rem(self.q + 3, 4), 2 * lax.rem(self.q + 1, 4)
        self.s_on = self.spread_on(10, self.slots, self.s_sent, lf, rt, self.along_second(1), self.along_second(3))

    def second_finish(self):
        for made in (*self.s_sent[2:], *self.s_on):
            made.wait_recv()
        own = 8 * self.c + 2 * self.p
        for s in range(2):
            self.out[own + s] = (self.slots[s] + self.slots[2 + s]) + (self.slots[4 + s] + self.slots[6 + s])

    def third_start(self):
        own = 8 * self.c + 2 * self.p
        self.t_sent = self.spread(16, self.out, own, self.along_first(1), self.along_first(3))
        part = self.out.at[pl.ds(own, 2)]
        self.to_sib = [self.copy(22, part, part, self.sibling())]

    def third_pass_on(self):
        h = 8 * self.c
        lf, rt = h + 2 * lax.rem(self.p + 3, 4), h + 2 * lax.rem(self.p + 1, 4)
        self.t_on = self.spread_on(16, self.out, self.t_sent, lf, rt, self.along_first(1), self.along_first(3))
        self.t_sent[2].wait_recv()
        part = self.out.at[pl.ds(lf, 2)]
        self.to_sib.append(self.copy(23, part, part, self.sibling()))
        self.t_sent[3].wait_recv()
        part = self.out.at[pl.ds(rt, 2)]
        self.to_sib.append(self.copy(24, part, part, self.sibling()))

    def third_finish(self):
        op = 8 * self.c + 2 * lax.rem(self.p + 2, 4)
        for s in range(2):
            self.t_on[s].wait_recv()
            part = self.out.at[op + s]
            self.to_sib.append(self.copy(25 + s, part, part, self.sibling()))

    def wait_sibling(self):
        for made in self.to_sib:
            made.wait_recv()

    def wait_sends(self):
        for made in self.started:
            made.wait_send()


def body(
    at_hbm, gt_hbm, e_hbm, q_hbm,
    merged_hbm, oo_ref, qq_ref, qn_ref, norm_ref,
    at, gt, e, q, qs, pt, lt, stage, gj, nb, qt,
    xs1, sib1, buf1, relay1, slots1, y1,
    xs2, sib2, buf2, relay2, slots2, y2,
    in_sem, stage_sem, send, recv, n_send, n_recv,
):
    z, x, c, y = (lax.axis_index(a) for a in (*DP, "mp"))
    pos = (z, x, c, y)
    loads = [
        pltpu.make_async_copy(q_hbm, q, in_sem.at[0]),
        pltpu.make_async_copy(gt_hbm, gt.at[pl.ds(0, TILE)], in_sem.at[1]),
        pltpu.make_async_copy(at_hbm, at.at[pl.ds(0, TILE)], in_sem.at[2]),
        pltpu.make_async_copy(e_hbm, e.at[pl.ds(0, TILE)], in_sem.at[3]),
    ]
    for load in loads:
        load.start()
    one = Sum(pos, (xs1, sib1, buf1, relay1, slots1, y1), (send, recv), 0)
    two = Sum(pos, (xs2, sib2, buf2, relay2, slots2, y2), (send, recv), N_MSG)

    barrier = pltpu.get_barrier_semaphore()
    peers = [one.along_first(1), one.along_first(3), one.along_second(1), one.along_second(3), one.sibling()]
    peers += [(z, x, c, lax.rem(y + d, 4)) for d in (1, 2, 3)]
    for peer in peers:
        pl.semaphore_signal(barrier, inc=1, device_id=peer, device_id_type=MESH)

    for ref in (at, gt, e):
        ref[pl.ds(TILE, PAD - TILE), :] = jnp.zeros((PAD - TILE, ref.shape[1]), BF16)

    loads[0].wait()
    hi, lo = split(q[...])
    qs[:, :RANK] = hi
    qs[:, RANK:] = lo
    for i in range(NCH):
        rows = min(CH, TILE - i * CH)
        t_hi, t_lo = split(q[pl.ds(i * CH, rows), :].T)
        lt[:RANK, pl.ds(i * CH, rows)] = t_hi
        lt[RANK:, pl.ds(i * CH, rows)] = t_lo
    lt[:, pl.ds(TILE, PAD - TILE)] = jnp.zeros((2 * RANK, PAD - TILE), BF16)
    loads[1].wait()

    def tokens(ref):
        for n in range(TOK // PIECE):
            cols = pl.ds(n * PIECE, PIECE)
            v = mm(lt[...], ref[:, cols])
            v_hi, v_lo = split(v[:RANK] + v[RANK:])
            pt[:RANK, cols] = v_hi
            pt[RANK:, cols] = v_lo

    tokens(gt)
    loads[2].wait()
    loads[3].wait()

    def left_piece(piece):
        rows = pl.ds(pl.multiple_of(piece * PIECE, PIECE), PIECE)
        v = mm(e[rows, :], qs[...]) + mm_t(at[rows, :], pt[...])
        v = v[:, :RANK] + v[:, RANK:]
        xs1[2 * piece] = v[:CH]
        xs1[2 * piece + 1] = v[CH:]

    def halves(total, compute):
        for n in range(4):
            compute(total.sibling_piece(n))
            if n == 0 and total is one:
                pl.semaphore_wait(barrier, len(peers))
            total.send_sibling(n)
        for n in range(4):
            compute(total.own_piece(n))
            total.own_ready(n)
            if n == 2:
                total.pass_on()

    halves(one, left_piece)

    stores = []

    def merged_rows(i):
        rows = min(PIECE, TILE - i * PIECE)
        slot = i % 2
        if i >= 2:
            stores[i - 2].wait()
        for n in range(8):
            cols = min(PIECE, TILE - n * PIECE)
            r, k = pl.ds(i * PIECE, rows), pl.ds(n * PIECE, cols)
            stage[slot, pl.ds(0, rows), k] = mm_t(at[r, :], gt[k, :]) + e[r, k].astype(F32)
        made = pltpu.make_async_copy(
            stage.at[slot, pl.ds(0, rows)], merged_hbm.at[pl.ds(i * PIECE, rows)], stage_sem.at[slot]
        )
        made.start()
        stores.append(made)

    merged_rows(0)
    one.finish_first()
    one.second_start()
    merged_rows(1)
    merged_rows(2)
    one.second_pass_on()
    merged_rows(3)
    one.second_finish()
    one.third_start()
    merged_rows(4)
    merged_rows(5)
    one.third_pass_on()
    merged_rows(6)
    one.third_finish()
    merged_rows(7)
    one.wait_sibling()

    for i in range(NCH):
        t_hi, t_lo = split(y1[i].T)
        lt[:RANK, pl.ds(i * CH, CH)] = t_hi
        lt[RANK:, pl.ds(i * CH, CH)] = t_lo
    tokens(at)

    def right_piece(piece):
        rows = pl.ds(pl.multiple_of(piece * PIECE, PIECE), PIECE)
        v = mm_t(pt[...], gt[rows, :])
        v = v[:RANK] + v[RANK:]
        xs2[2 * piece] = v[:, :CH]
        xs2[2 * piece + 1] = v[:, CH:]

        @pl.when(piece < 7)
        def _():
            w = mm(lt[...], e[:, rows])
            w = w[:RANK] + w[RANK:]
            xs2[2 * piece] += w[:, :CH]
            xs2[2 * piece + 1] += w[:, CH:]

        @pl.when(piece == 7)
        def _():
            w = mm(lt[...], e[:, pl.ds(7 * PIECE, TILE - 7 * PIECE)])
            w = w[:RANK] + w[RANK:]
            xs2[14] += w[:, :CH]
            xs2[15, :, pl.ds(0, CH // 2)] += w[:, CH:]

    halves(two, right_piece)

    left = y1[...].reshape(PAD, RANK)
    row_i = lax.broadcasted_iota(jnp.int32, (RANK, RANK), 0)
    col_i = lax.broadcasted_iota(jnp.int32, (RANK, RANK), 1)
    gj[:, :RANK] = lax.dot_general(left, left, (((0,), (0,)), ((), ())), precision=PRECISE, preferred_element_type=F32)
    gj[:, RANK:] = jnp.where(row_i == col_i, 1.0, 0.0)

    def eliminate(first, count):
        def step(k, carry):
            row = gj[pl.ds(k, 1), :]
            whole = gj[...]
            pivot = jnp.sum(jnp.where(col_i[:1] == k, row[:, :RANK], 0.0), axis=1, keepdims=True)
            column = jnp.sum(jnp.where(col_i == k, whole[:, :RANK], 0.0), axis=1, keepdims=True)
            factor = jnp.where(row_i[:, :1] > k, column / pivot, 0.0)
            gj[...] = whole - factor * row
            return carry

        lax.fori_loop(first, first + count, step, 0)

    two.finish_first()
    two.second_start()
    eliminate(0, 32)
    two.second_pass_on()
    eliminate(32, 24)
    two.second_finish()
    two.third_start()
    eliminate(56, 32)
    two.third_pass_on()
    eliminate(88, 24)
    two.third_finish()
    eliminate(112, 16)
    diagonal = jnp.sum(jnp.where(row_i == col_i, gj[:, :RANK], 0.0), axis=1, keepdims=True)
    inverse = gj[:, RANK:] / jnp.sqrt(diagonal)

    for i in range(NCH):
        rows = min(CH, TILE - i * CH)
        o = lax.dot_general(y1[i], inverse, (((1,), (1,)), ((), ())), precision=PRECISE, preferred_element_type=F32)
        o_hi, o_lo = split(o[:rows])
        r = pl.ds(i * CH, rows)
        oo_ref[r, :RANK] = o_hi
        oo_ref[r, RANK : 2 * RANK] = o_hi
        oo_ref[r, 2 * RANK :] = o_lo
    two.wait_sibling()

    total = jnp.zeros((RANK, CH), F32)
    scaled = inverse / 32.0
    for i in range(NCH):
        rows = min(CH, TILE - i * CH)
        t = jnp.dot(scaled, y2[i], precision=PRECISE, preferred_element_type=F32)
        total = total + t * t
        qt[i] = t
        t_hi, t_lo = split(t[:, :rows])
        k = pl.ds(i * CH, rows)
        qq_ref[:RANK, k] = t_hi
        qq_ref[RANK : 2 * RANK, k] = t_lo
        qq_ref[2 * RANK :, k] = t_hi
    nb[y] = jnp.broadcast_to(jnp.sum(total), (8, RANK))
    gone = []
    for d in (1, 2, 3):
        made = pltpu.make_async_remote_copy(
            src_ref=nb.at[y],
            dst_ref=nb.at[y],
            send_sem=n_send.at[d - 1],
            recv_sem=n_recv.at[d - 1],
            device_id=(z, x, c, lax.rem(y + d, 4)),
            device_id_type=MESH,
        )
        made.start()
        gone.append(made)
    for i in range(NCH):
        rows = min(CH, TILE - i * CH)
        qn_ref[pl.ds(i * CH, rows), :] = qt[i].T[:rows]
    for made in stores[-2:]:
        made.wait()
    one.wait_sends()
    two.wait_sends()
    for made in gone:
        made.wait()
    norm_ref[...] = (nb[0] + nb[1]) + (nb[2] + nb[3])


def compress(at, gt, error, q):
    any_spec = pl.BlockSpec(memory_space=pl.ANY)
    vmem = pl.BlockSpec(memory_space=pltpu.VMEM)
    chunks = lambda n: pltpu.VMEM((n, CH, RANK), F32)
    sums = [chunks(NCH), pltpu.VMEM((4, 2, CH, RANK), F32), chunks(6), chunks(2), chunks(8), chunks(NCH)]
    return pl.pallas_call(
        body,
        out_shape=(
            jax.ShapeDtypeStruct((TILE, TILE), F32),
            jax.ShapeDtypeStruct((TILE, 3 * RANK), BF16),
            jax.ShapeDtypeStruct((3 * RANK, TILE), BF16),
            jax.ShapeDtypeStruct((TILE, RANK), F32),
            jax.ShapeDtypeStruct((8, RANK), F32),
        ),
        in_specs=[any_spec] * 4,
        out_specs=(any_spec, vmem, vmem, vmem, vmem),
        scratch_shapes=[
            pltpu.VMEM((PAD, TOK), BF16),
            pltpu.VMEM((PAD, TOK), BF16),
            pltpu.VMEM((PAD, TILE), BF16),
            pltpu.VMEM((TILE, RANK), F32),
            pltpu.VMEM((TILE, 2 * RANK), BF16),
            pltpu.VMEM((2 * RANK, TOK), BF16),
            pltpu.VMEM((2 * RANK, PAD), BF16),
            pltpu.VMEM((2, PIECE, TILE), F32),
            pltpu.VMEM((RANK, 2 * RANK), F32),
            pltpu.VMEM((4, 8, RANK), F32),
            chunks(NCH),
            *sums,
            *sums,
            pltpu.SemaphoreType.DMA((4,)),
            pltpu.SemaphoreType.DMA((2,)),
            pltpu.SemaphoreType.DMA((2 * N_MSG,)),
            pltpu.SemaphoreType.DMA((2 * N_MSG,)),
            pltpu.SemaphoreType.DMA((3,)),
            pltpu.SemaphoreType.DMA((3,)),
        ],
        compiler_params=pltpu.CompilerParams(
            collective_id=0, has_side_effects=True, vmem_limit_bytes=56 * 1024 * 1024
        ),
        name="compress",
    )(at, gt, error, q)


def residual(merged, oo, qq):
    def block(m_ref, o_ref, q_ref, out_ref):
        for n in range(8):
            k = pl.ds(n * PIECE, min(PIECE, TILE - n * PIECE))
            out_ref[:, k] = (m_ref[:, k] - mm(o_ref[...], q_ref[:, k])).astype(BF16)

    rows = TILE // 4
    return pl.pallas_call(
        block,
        grid=(4,),
        out_shape=jax.ShapeDtypeStruct((TILE, TILE), BF16),
        in_specs=[
            pl.BlockSpec((rows, TILE), lambda i: (i, 0)),
            pl.BlockSpec((rows, 3 * RANK), lambda i: (i, 0)),
            pl.BlockSpec((3 * RANK, TILE), lambda i: (0, 0)),
        ],
        out_specs=pl.BlockSpec((rows, TILE), lambda i: (i, 0)),
        name="residual",
    )(merged, oo, qq)


def per_device(acts, grads, error, momentum, q_start):
    at, gt = acts[:, 0, :].T, grads[:, 0, :].T
    merged, oo, qq, q_tile, norm = compress(at, gt, error[0, 0], q_start[0])
    error_next = residual(merged, oo, qq)
    rms_value = jnp.sqrt(norm[0, 0] / (D * D))
    owned_rows = momentum.shape[1]
    basis_owned = lax.dynamic_slice_in_dim(oo, lax.axis_index(DP) * owned_rows, owned_rows, 0)
    update = jnp.dot(basis_owned, qq, preferred_element_type=F32)
    momentum_next = 0.9 * momentum[0] + 0.1 * update / (rms_value + 1e-06)
    return (error_next[None, None], momentum_next[None], q_tile[None])


def solution(mesh):
    split_mesh = Mesh(mesh.devices.reshape(4, 4, 2, mesh.shape["mp"]), (*DP, "mp"))
    in_specs = (
        P(DP, "mp", None),
        P(DP, "mp", None),
        P(DP, "mp", None, None),
        P("mp", DP, None),
        P("mp", None, None),
    )
    out_specs = (P(DP, "mp", None, None), P("mp", DP, None), P("mp", None, None))
    return jax.shard_map(
        per_device, mesh=split_mesh, in_specs=in_specs, out_specs=out_specs, check_vma=False
    )
```

```python
import jax
import jax.numpy as jnp
from jax import lax
from jax.experimental import pallas as pl
from jax.experimental.pallas import tpu as pltpu
from jax.sharding import Mesh
from jax.sharding import PartitionSpec as P

D = 3968
DP = ("dp_0", "dp_1", "dp_2")
MESH = pl.DeviceIdType.MESH
TILE = 1984
PAD = 2048
RANK = 128
TOK = 768
CH = 128
NCH = 16
PIECE = 256
F32 = jnp.float32
BF16 = jnp.bfloat16
PRECISE = lax.Precision.HIGHEST
ORDER = (2, 1, 3, 0)
N_MSG = 27
OWNED = 62


def mm(a, b):
    return jnp.dot(a, b, preferred_element_type=F32)


def mm_t(a, b):
    return lax.dot_general(a, b, (((1,), (1,)), ((), ())), preferred_element_type=F32)


def split(v):
    hi = v.astype(BF16)
    return hi, (v - hi.astype(F32)).astype(BF16)


class Sum:
    def __init__(self, pos, bufs, sems, base):
        self.z, self.x, self.c, self.y = pos
        self.xs, self.sib, self.buf, self.relay, self.slots, self.out = bufs
        self.send, self.recv = sems
        self.base = base
        self.started = []
        z, x, c = self.z, self.x, self.c
        self.p = (1 - c) * x + c * z
        self.q = (1 - c) * z + c * x
        self.other_p = c * x + (1 - c) * z

    def along_first(self, d):
        return (lax.rem(self.z + self.c * d, 4), lax.rem(self.x + (1 - self.c) * d, 4), self.c, self.y)

    def along_second(self, d):
        return (lax.rem(self.z + (1 - self.c) * d, 4), lax.rem(self.x + self.c * d, 4), self.c, self.y)

    def sibling(self):
        return (self.z, self.x, 1 - self.c, self.y)

    def copy(self, i, src, dst, to):
        made = pltpu.make_async_remote_copy(
            src_ref=src,
            dst_ref=dst,
            send_sem=self.send.at[self.base + i],
            recv_sem=self.recv.at[self.base + i],
            device_id=to,
            device_id_type=MESH,
        )
        made.start()
        self.started.append(made)
        return made

    def sibling_piece(self, n):
        pos = lax.rem(self.other_p + ORDER[n], 4)
        return 4 * (1 - self.c) + pos

    def own_piece(self, n):
        return 4 * self.c + lax.rem(self.p + ORDER[n], 4)

    def send_sibling(self, n):
        i = 2 * self.sibling_piece(n)
        self.from_sibling = getattr(self, "from_sibling", {})
        self.from_sibling[n] = self.copy(n, self.xs.at[pl.ds(i, 2)], self.sib.at[n], self.sibling())

    def own_ready(self, n):
        i = 2 * self.own_piece(n)
        self.from_sibling[n].wait_recv()
        for s in range(2):
            self.xs[i + s] = self.xs[i + s] + self.sib[n, s]
        right, left = self.along_first(1), self.along_first(3)
        if n == 0:
            self.a_r = self.copy(4, self.xs.at[i], self.buf.at[0], right)
            self.a_l = self.copy(5, self.xs.at[i + 1], self.buf.at[1], left)
        elif n == 1:
            self.d_r = self.copy(6, self.xs.at[i + 1], self.buf.at[2], right)
        elif n == 2:
            self.d_l = self.copy(7, self.xs.at[i], self.buf.at[3], left)

    def pass_on(self):
        right, left = self.along_first(1), self.along_first(3)
        self.a_r.wait_recv()
        self.relay[0] = self.xs[2 * self.own_piece(1)] + self.buf[0]
        self.b_r = self.copy(8, self.relay.at[0], self.buf.at[4], right)
        self.a_l.wait_recv()
        self.relay[1] = self.xs[2 * self.own_piece(2) + 1] + self.buf[1]
        self.b_l = self.copy(9, self.relay.at[1], self.buf.at[5], left)

    def finish_first(self):
        i = 2 * self.own_piece(3)
        self.b_r.wait_recv()
        self.d_l.wait_recv()
        self.slots[2 * self.q] = self.xs[i] + self.buf[4] + self.buf[3]
        self.d_r.wait_recv()
        self.b_l.wait_recv()
        self.slots[2 * self.q + 1] = self.xs[i + 1] + self.buf[2] + self.buf[5]

    def spread(self, base, ref, at, right, left):
        own = ref.at[at], ref.at[at + 1]
        r0 = self.copy(base, own[0], own[0], right)
        l1 = self.copy(base + 1, own[1], own[1], left)
        r1 = self.copy(base + 2, own[1], own[1], right)
        l0 = self.copy(base + 3, own[0], own[0], left)
        return r0, l1, r1, l0

    def spread_on(self, base, ref, sent, from_left, from_right, right, left):
        r0, l1, _, _ = sent
        r0.wait_recv()
        f_r = self.copy(base + 4, ref.at[from_left], ref.at[from_left], right)
        l1.wait_recv()
        f_l = self.copy(base + 5, ref.at[from_right + 1], ref.at[from_right + 1], left)
        return f_r, f_l

    def second_start(self):
        self.s_sent = self.spread(10, self.slots, 2 * self.q, self.along_second(1), self.along_second(3))

    def second_pass_on(self):
        lf, rt = 2 * lax.rem(self.q + 3, 4), 2 * lax.rem(self.q + 1, 4)
        self.s_on = self.spread_on(10, self.slots, self.s_sent, lf, rt, self.along_second(1), self.along_second(3))

    def second_finish(self, change):
        for made in (*self.s_sent[2:], *self.s_on):
            made.wait_recv()
        own = 8 * self.c + 2 * self.p
        for s in range(2):
            self.out[own + s] = change(
                (self.slots[s] + self.slots[2 + s]) + (self.slots[4 + s] + self.slots[6 + s])
            )

    def third_start(self):
        own = 8 * self.c + 2 * self.p
        self.t_sent = self.spread(16, self.out, own, self.along_first(1), self.along_first(3))
        part = self.out.at[pl.ds(own, 2)]
        self.to_sib = [self.copy(22, part, part, self.sibling())]

    def third_pass_on(self):
        h = 8 * self.c
        lf, rt = h + 2 * lax.rem(self.p + 3, 4), h + 2 * lax.rem(self.p + 1, 4)
        self.t_on = self.spread_on(16, self.out, self.t_sent, lf, rt, self.along_first(1), self.along_first(3))
        self.t_sent[2].wait_recv()
        part = self.out.at[pl.ds(lf, 2)]
        self.to_sib.append(self.copy(23, part, part, self.sibling()))
        self.t_sent[3].wait_recv()
        part = self.out.at[pl.ds(rt, 2)]
        self.to_sib.append(self.copy(24, part, part, self.sibling()))

    def third_finish(self):
        op = 8 * self.c + 2 * lax.rem(self.p + 2, 4)
        for s in range(2):
            self.t_on[s].wait_recv()
            part = self.out.at[op + s]
            self.to_sib.append(self.copy(25 + s, part, part, self.sibling()))

    def wait_sibling(self):
        for made in self.to_sib:
            made.wait_recv()

    def wait_sends(self):
        for made in self.started:
            made.wait_send()


def body(
    at_hbm, gt_hbm, e_hbm, q_hbm,
    merged_ref, oo_ref, qq_ref, qn_ref, own_ref, norm_ref,
    at, gt, e, ep, q, qs, pt, lt, gj, of, nb, ns,
    xs1, sib1, buf1, relay1, slots1, y1,
    xs2, sib2, buf2, relay2, slots2, y2,
    in_sem, send, recv, n_send, n_recv,
):
    z, x, c, y = (lax.axis_index(a) for a in (*DP, "mp"))
    pos = (z, x, c, y)
    half = PAD // 2
    loads = [
        pltpu.make_async_copy(q_hbm, q, in_sem.at[0]),
        pltpu.make_async_copy(gt_hbm, gt.at[pl.ds(0, TILE)], in_sem.at[1]),
        pltpu.make_async_copy(at_hbm, at.at[pl.ds(0, TILE)], in_sem.at[2]),
    ]
    low = pltpu.make_async_copy(e_hbm.at[pl.ds(0, half)], e.at[pl.ds(0, half)], in_sem.at[3])
    high = pltpu.make_async_copy(e_hbm.at[pl.ds(half, TILE - half)], e.at[pl.ds(half, TILE - half)], in_sem.at[4])
    for load in loads:
        load.start()

    def by_core(first, second):
        pl.when(c == 0)(first)
        pl.when(c == 1)(second)

    by_core(high.start, low.start)
    by_core(low.start, high.start)
    one = Sum(pos, (xs1, sib1, buf1, relay1, slots1, y1), (send, recv), 0)
    two = Sum(pos, (xs2, sib2, buf2, relay2, slots2, y2), (send, recv), N_MSG)

    def plane(d, f):
        return (*one.along_first(d)[:3], lax.rem(y + f, 4))

    steps = [(d, f) for d in range(4) for f in range(4) if d or f]
    barrier = pltpu.get_barrier_semaphore()
    peers = [one.along_second(1), one.along_second(3), one.sibling(), *(plane(d, f) for d, f in steps)]
    for peer in peers:
        pl.semaphore_signal(barrier, inc=1, device_id=peer, device_id_type=MESH)

    for ref in (at, gt, e, ep):
        ref[pl.ds(TILE, PAD - TILE), :] = jnp.zeros((PAD - TILE, ref.shape[1]), BF16)
    ep[:, pl.ds(TILE, PAD - TILE)] = jnp.zeros((PAD, PAD - TILE), BF16)

    loads[0].wait()
    hi, lo = split(q[...])
    qs[:, :RANK] = hi
    qs[:, RANK:] = lo
    for i in range(NCH):
        rows = min(CH, TILE - i * CH)
        t_hi, t_lo = split(q[pl.ds(i * CH, rows), :].T)
        lt[:RANK, pl.ds(i * CH, rows)] = t_hi
        lt[RANK:, pl.ds(i * CH, rows)] = t_lo
    lt[:, pl.ds(TILE, PAD - TILE)] = jnp.zeros((2 * RANK, PAD - TILE), BF16)
    loads[1].wait()

    def tokens(ref):
        for n in range(TOK // PIECE):
            cols = pl.ds(n * PIECE, PIECE)
            v = mm(lt[...], ref[:, cols])
            v_hi, v_lo = split(v[:RANK] + v[RANK:])
            pt[:RANK, cols] = v_hi
            pt[RANK:, cols] = v_lo

    tokens(gt)
    loads[2].wait()
    by_core(high.wait, low.wait)

    def place(piece):
        return pl.ds(pl.multiple_of(piece * PIECE, PIECE), PIECE)

    def left_pieces(*pieces):
        done = [mm(e[place(i), :], qs[...]) + mm_t(at[place(i), :], pt[...]) for i in pieces]
        for piece, v in zip(pieces, done):
            v = v[:, :RANK] + v[:, RANK:]
            xs1[2 * piece] = v[:CH]
            xs1[2 * piece + 1] = v[CH:]

    def halves(total, compute, between):
        for n in (0, 2):
            compute(total.sibling_piece(n), total.sibling_piece(n + 1))
            if n == 0 and total is one:
                pl.semaphore_wait(barrier, len(peers))
            total.send_sibling(n)
            total.send_sibling(n + 1)
        between()
        compute(total.own_piece(0), total.own_piece(1))
        total.own_ready(0)
        total.own_ready(1)
        compute(total.own_piece(2), total.own_piece(3))
        total.own_ready(2)
        total.pass_on()
        total.own_ready(3)

    halves(one, left_pieces, lambda: by_core(low.wait, high.wait))

    def merged_rows(i):
        r = pl.ds(i * PIECE, min(PIECE, TILE - i * PIECE))
        for n in range(8):
            k = pl.ds(n * PIECE, min(PIECE, TILE - n * PIECE))
            stored = e[r, k]
            ep[r, k] = stored
            merged_ref[r, k] = mm_t(at[r, :], gt[k, :]) + stored.astype(F32)

    merged_rows(0)
    one.finish_first()
    one.second_start()
    merged_rows(1)
    merged_rows(2)
    one.second_pass_on()
    merged_rows(3)
    merged_rows(4)
    one.second_finish(lambda v: v)
    one.third_start()
    merged_rows(5)
    merged_rows(6)
    one.third_pass_on()
    merged_rows(7)
    one.third_finish()
    one.wait_sibling()

    for i in range(NCH):
        t_hi, t_lo = split(y1[i].T)
        lt[:RANK, pl.ds(i * CH, CH)] = t_hi
        lt[RANK:, pl.ds(i * CH, CH)] = t_lo
    tokens(at)

    def right_pieces(*pieces):
        done = [mm(lt[...], ep[:, place(i)]) + mm_t(pt[...], gt[place(i), :]) for i in pieces]
        for piece, v in zip(pieces, done):
            v = v[:RANK] + v[RANK:]
            xs2[2 * piece] = v[:, :CH]
            xs2[2 * piece + 1] = v[:, CH:]

    halves(two, right_pieces, lambda: None)

    left = y1[...].reshape(PAD, RANK)
    row_i = lax.broadcasted_iota(jnp.int32, (RANK, RANK), 0)
    col_i = lax.broadcasted_iota(jnp.int32, (RANK, RANK), 1)
    gj[:, :RANK] = lax.dot_general(left, left, (((0,), (0,)), ((), ())), precision=PRECISE, preferred_element_type=F32)
    gj[:, RANK:] = jnp.where(row_i == col_i, 1.0, 0.0)

    def eliminate(first, count):
        def step(k, carry):
            row = gj[pl.ds(k, 1), :]
            whole = gj[...]
            pivot = jnp.sum(jnp.where(col_i[:1] == k, row[:, :RANK], 0.0), axis=1, keepdims=True)
            column = jnp.sum(jnp.where(col_i == k, whole[:, :RANK], 0.0), axis=1, keepdims=True)
            factor = jnp.where(row_i[:, :1] > k, column / pivot, 0.0)
            gj[...] = whole - factor * row
            return carry

        lax.fori_loop(first, first + count, step, 0)

    eliminate(0, 28)
    two.finish_first()
    two.second_start()
    eliminate(28, 48)
    two.second_pass_on()
    eliminate(76, 52)
    diagonal = jnp.sum(jnp.where(row_i == col_i, gj[:, :RANK], 0.0), axis=1, keepdims=True)
    inverse = gj[:, RANK:] / jnp.sqrt(diagonal)
    scaled = inverse / 32.0
    squares = []

    def to_q(v):
        t = jnp.dot(scaled, v, precision=PRECISE, preferred_element_type=F32)
        squares.append(t * t)
        return t

    two.second_finish(to_q)
    two.third_start()

    mine = 4 * one.p + y
    nb[mine] = jnp.broadcast_to(jnp.sum(squares[0] + squares[1]), (8, RANK))
    gone = []

    def exchange(i, ref, to):
        made = pltpu.make_async_remote_copy(
            src_ref=ref,
            dst_ref=ref,
            send_sem=n_send.at[i],
            recv_sem=n_recv.at[i],
            device_id=to,
            device_id_type=MESH,
        )
        made.start()
        gone.append(made)

    for i, (d, f) in enumerate(steps):
        exchange(i, nb.at[mine], plane(d, f))

    def ortho(first, count):
        for i in range(first, first + count):
            rows = min(CH, TILE - i * CH)
            o = lax.dot_general(
                y1[i], inverse, (((1,), (1,)), ((), ())), precision=PRECISE, preferred_element_type=F32
            )
            of[pl.ds(i * CH, CH), :] = o
            o_hi, o_lo = split(o[:rows])
            r = pl.ds(i * CH, rows)
            oo_ref[r, :RANK] = o_hi
            oo_ref[r, RANK : 2 * RANK] = o_hi
            oo_ref[r, 2 * RANK :] = o_lo

    ortho(0, 8)
    two.third_pass_on()
    ortho(8, 8)
    for made in gone:
        made.wait_recv()
    norm = nb[0]
    for i in range(1, 16):
        norm = norm + nb[i]
    ns[c] = norm
    exchange(len(steps), ns.at[c], one.sibling())
    two.third_finish()
    o_hi, o_lo = split(of[pl.ds(((z * 4 + x) * 2 + c) * OWNED, 64), :])
    own_ref[:, :RANK] = o_hi
    own_ref[:, RANK : 2 * RANK] = o_hi
    own_ref[:, 2 * RANK :] = o_lo
    one.wait_sends()
    gone[-1].wait_recv()
    norm_ref[...] = ns[0] + ns[1]
    two.wait_sibling()
    for i in range(NCH):
        rows = min(CH, TILE - i * CH)
        t = y2[i]
        t_hi, t_lo = split(t[:, :rows])
        k = pl.ds(i * CH, rows)
        qq_ref[:RANK, k] = t_hi
        qq_ref[RANK : 2 * RANK, k] = t_lo
        qq_ref[2 * RANK :, k] = t_hi
        qn_ref[k, :] = t.T[:rows]
    two.wait_sends()
    for made in gone:
        made.wait_send()


def compress(at, gt, error, q):
    any_spec = pl.BlockSpec(memory_space=pl.ANY)
    vmem = pl.BlockSpec(memory_space=pltpu.VMEM)
    chunks = lambda n: pltpu.VMEM((n, CH, RANK), F32)
    sums = [chunks(NCH), pltpu.VMEM((4, 2, CH, RANK), F32), chunks(6), chunks(2), chunks(8), chunks(NCH)]
    return pl.pallas_call(
        body,
        out_shape=(
            pltpu.VMEM((TILE, TILE), F32),
            pltpu.VMEM((TILE, 3 * RANK), BF16),
            pltpu.VMEM((3 * RANK, TILE), BF16),
            pltpu.VMEM((TILE, RANK), F32),
            pltpu.VMEM((64, 3 * RANK), BF16),
            pltpu.VMEM((8, RANK), F32),
        ),
        in_specs=[any_spec] * 4,
        out_specs=(vmem,) * 6,
        scratch_shapes=[
            pltpu.VMEM((PAD, TOK), BF16),
            pltpu.VMEM((PAD, TOK), BF16),
            pltpu.VMEM((PAD, TILE), BF16),
            pltpu.VMEM((PAD, PAD), BF16),
            pltpu.VMEM((TILE, RANK), F32),
            pltpu.VMEM((TILE, 2 * RANK), BF16),
            pltpu.VMEM((2 * RANK, TOK), BF16),
            pltpu.VMEM((2 * RANK, PAD), BF16),
            pltpu.VMEM((RANK, 2 * RANK), F32),
            pltpu.VMEM((PAD, RANK), F32),
            pltpu.VMEM((16, 8, RANK), F32),
            pltpu.VMEM((2, 8, RANK), F32),
            *sums,
            *sums,
            pltpu.SemaphoreType.DMA((5,)),
            pltpu.SemaphoreType.DMA((2 * N_MSG,)),
            pltpu.SemaphoreType.DMA((2 * N_MSG,)),
            pltpu.SemaphoreType.DMA((16,)),
            pltpu.SemaphoreType.DMA((16,)),
        ],
        compiler_params=pltpu.CompilerParams(
            collective_id=0, has_side_effects=True, vmem_limit_bytes=42 * 1024 * 1024
        ),
        name="compress",
    )(at, gt, error, q)


def finish(merged, oo, qq, qn, own, norm, momentum):
    rows = TILE // 4

    def block(m_ref, o_ref, q_ref, n_ref, own_ref, norm_ref, mom_ref, out_ref, next_ref, qn_ref):
        i = pl.program_id(0)
        at = pl.ds(pl.multiple_of(i * rows, 16), rows)
        columns = [pl.ds(n * PIECE, min(PIECE, TILE - n * PIECE)) for n in range(8)]
        for k in columns:
            out_ref[:, k] = (m_ref[at, k] - mm(o_ref[at, :], q_ref[:, k])).astype(BF16)
        qn_ref[...] = n_ref[at, :]

        @pl.when(i == 0)
        def _():
            rms = jnp.sqrt(norm_ref[:1, :1] / (D * D))
            scale = 0.1 / (rms + 1e-6)
            for k in columns:
                next_ref[:, k] = 0.9 * mom_ref[:, k] + scale * mm(own_ref[...], q_ref[:, k])[:OWNED]

    vmem = pl.BlockSpec(memory_space=pltpu.VMEM)
    held = [pltpu.with_memory_space_constraint(v, pltpu.VMEM) for v in (merged, oo, qq, qn, own, norm)]
    whole = pl.BlockSpec((OWNED, TILE), lambda i: (0, 0))
    return pl.pallas_call(
        block,
        grid=(4,),
        out_shape=(
            jax.ShapeDtypeStruct((TILE, TILE), BF16),
            jax.ShapeDtypeStruct((OWNED, TILE), F32),
            jax.ShapeDtypeStruct((TILE, RANK), F32),
        ),
        in_specs=[vmem] * 6 + [whole],
        out_specs=(
            pl.BlockSpec((rows, TILE), lambda i: (i, 0)),
            whole,
            pl.BlockSpec((rows, RANK), lambda i: (i, 0)),
        ),
        compiler_params=pltpu.CompilerParams(vmem_limit_bytes=16 * 1024 * 1024),
        name="finish",
    )(*held, momentum)


def per_device(acts, grads, error, momentum, q_start):
    at, gt = acts[:, 0, :].T, grads[:, 0, :].T
    made = compress(at, gt, error[0, 0], q_start[0])
    error_next, momentum_next, q_tile = finish(*made, momentum[0])
    return (error_next[None, None], momentum_next[None], q_tile[None])


def solution(mesh):
    split_mesh = Mesh(mesh.devices.reshape(4, 4, 2, mesh.shape["mp"]), (*DP, "mp"))
    in_specs = (
        P(DP, "mp", None),
        P(DP, "mp", None),
        P(DP, "mp", None, None),
        P("mp", DP, None),
        P("mp", None, None),
    )
    out_specs = (P(DP, "mp", None, None), P("mp", DP, None), P("mp", None, None))
    return jax.shard_map(
        per_device, mesh=split_mesh, in_specs=in_specs, out_specs=out_specs, check_vma=False
    )
```

```python
import jax
import jax.numpy as jnp
from jax import lax
from jax.experimental import pallas as pl
from jax.experimental.pallas import tpu as pltpu
from jax.sharding import Mesh
from jax.sharding import PartitionSpec as P

D = 3968
DP = ("dp_0", "dp_1", "dp_2")
MESH = pl.DeviceIdType.MESH
TILE = 1984
PAD = 2048
RANK = 128
TOK = 768
CH = 128
NCH = 16
PIECE = 256
F32 = jnp.float32
BF16 = jnp.bfloat16
PRECISE = lax.Precision.HIGHEST
ORDER = (2, 1, 3, 0)
CHIPS = [(z, x) for z in ORDER for x in ORDER if z or x]
N_MSG = 35
OWNED = 62


def mm(a, b):
    return jnp.dot(a, b, preferred_element_type=F32)


def mm_t(a, b):
    return lax.dot_general(a, b, (((1,), (1,)), ((), ())), preferred_element_type=F32)


def split(v):
    hi = v.astype(BF16)
    return hi, (v - hi.astype(F32)).astype(BF16)


class Sum:
    def __init__(self, pos, bufs, sems, base):
        self.z, self.x, self.c, self.y = pos
        self.xs, self.sib, self.slots, self.out = bufs
        self.send, self.recv = sems
        self.base = base
        self.started = []
        self.r = 4 * self.z + self.x
        self.from_sibling, self.scattered, self.spread = {}, [], []

    def chip(self, dz, dx):
        return lax.rem(self.z + dz, 4), lax.rem(self.x + dx, 4)

    def sibling(self):
        return (self.z, self.x, 1 - self.c, self.y)

    def copy(self, i, src, dst, to):
        made = pltpu.make_async_remote_copy(
            src_ref=src,
            dst_ref=dst,
            send_sem=self.send.at[self.base + i],
            recv_sem=self.recv.at[self.base + i],
            device_id=to,
            device_id_type=MESH,
        )
        made.start()
        self.started.append(made)
        return made

    def sibling_piece(self, n):
        return 4 * (1 - self.c) + lax.rem(self.z + ORDER[n], 4)

    def own_piece(self, n):
        return 4 * self.c + lax.rem(self.z + ORDER[n], 4)

    def send_sibling(self, n):
        i = 4 * self.sibling_piece(n)
        self.from_sibling[n] = self.copy(n, self.xs.at[pl.ds(i, 4)], self.sib.at[n], self.sibling())

    def own_ready(self, n):
        i = pl.ds(4 * self.own_piece(n), 4)
        self.from_sibling[n].wait_recv()
        self.xs[i] = self.xs[i] + self.sib[n]
        for dx in ORDER:
            if not (ORDER[n] or dx):
                continue
            z, x = self.chip(ORDER[n], dx)
            made = self.copy(
                4 + len(self.scattered),
                self.xs.at[16 * self.c + 4 * z + x],
                self.slots.at[self.r],
                (z, x, self.c, self.y),
            )
            self.scattered.append(made)

    def finish_scatter(self, change):
        mine = 16 * self.c + self.r
        self.slots[self.r] = self.xs[mine]
        for made in self.scattered:
            made.wait_recv()
        total = self.slots[0]
        for i in range(1, 16):
            total = total + self.slots[i]
        self.out[mine] = change(total)
        part = self.out.at[mine]
        for n, (dz, dx) in enumerate(CHIPS):
            self.spread.append(self.copy(19 + n, part, part, (*self.chip(dz, dx), self.c, self.y)))

    def finish_spread(self):
        for made in self.spread:
            made.wait_recv()
        part = self.out.at[pl.ds(16 * self.c, 16)]
        self.to_sibling = self.copy(34, part, part, self.sibling())

    def wait_sibling(self):
        self.to_sibling.wait_recv()

    def wait_sends(self):
        for made in self.started:
            made.wait_send()


def body(
    at_hbm, gt_hbm, e_hbm, q_hbm,
    merged_ref, oo_ref, qq_ref, qn_ref, own_ref, norm_ref,
    at, gt, e, ep, q, qs, pt, lt, gj, of, nt, nb, ns,
    xs1, sib1, slots1, y1,
    xs2, sib2, slots2, y2,
    in_sem, send, recv, n_send, n_recv,
):
    z, x, c, y = (lax.axis_index(a) for a in (*DP, "mp"))
    pos = (z, x, c, y)
    half = PAD // 2
    loads = [
        pltpu.make_async_copy(q_hbm, q, in_sem.at[0]),
        pltpu.make_async_copy(gt_hbm, gt.at[pl.ds(0, TILE)], in_sem.at[1]),
        pltpu.make_async_copy(at_hbm, at.at[pl.ds(0, TILE)], in_sem.at[2]),
    ]
    low = pltpu.make_async_copy(e_hbm.at[pl.ds(0, half)], e.at[pl.ds(0, half)], in_sem.at[3])
    high = pltpu.make_async_copy(e_hbm.at[pl.ds(half, TILE - half)], e.at[pl.ds(half, TILE - half)], in_sem.at[4])
    for load in loads:
        load.start()

    def by_core(first, second):
        pl.when(c == 0)(first)
        pl.when(c == 1)(second)

    by_core(high.start, low.start)
    by_core(low.start, high.start)
    one = Sum(pos, (xs1, sib1, slots1, y1), (send, recv), 0)
    two = Sum(pos, (xs2, sib2, slots2, y2), (send, recv), N_MSG)

    tiles = [(z, x, c, lax.rem(y + d, 4)) for d in (1, 2, 3)]
    chips = [(*one.chip(dz, dx), c, y) for dz, dx in CHIPS]
    barrier = pltpu.get_barrier_semaphore()
    peers = [one.sibling(), *tiles, *chips]
    for peer in peers:
        pl.semaphore_signal(barrier, inc=1, device_id=peer, device_id_type=MESH)

    for ref in (at, gt, e, ep):
        ref[pl.ds(TILE, PAD - TILE), :] = jnp.zeros((PAD - TILE, ref.shape[1]), BF16)
    ep[:, pl.ds(TILE, PAD - TILE)] = jnp.zeros((PAD, PAD - TILE), BF16)

    loads[0].wait()
    hi, lo = split(q[...])
    qs[:, :RANK] = hi
    qs[:, RANK:] = lo
    for i in range(NCH):
        rows = min(CH, TILE - i * CH)
        t_hi, t_lo = split(q[pl.ds(i * CH, rows), :].T)
        lt[:RANK, pl.ds(i * CH, rows)] = t_hi
        lt[RANK:, pl.ds(i * CH, rows)] = t_lo
    lt[:, pl.ds(TILE, PAD - TILE)] = jnp.zeros((2 * RANK, PAD - TILE), BF16)
    loads[1].wait()

    def tokens(ref):
        for n in range(TOK // PIECE):
            cols = pl.ds(n * PIECE, PIECE)
            v = mm(lt[...], ref[:, cols])
            v_hi, v_lo = split(v[:RANK] + v[RANK:])
            pt[:RANK, cols] = v_hi
            pt[RANK:, cols] = v_lo

    tokens(gt)
    loads[2].wait()
    by_core(high.wait, low.wait)

    def place(piece):
        return pl.ds(pl.multiple_of(piece * PIECE, PIECE), PIECE)

    def left_pieces(*pieces):
        done = [mm(e[place(i), :], qs[...]) + mm_t(at[place(i), :], pt[...]) for i in pieces]
        for piece, v in zip(pieces, done):
            v = v[:, :RANK] + v[:, RANK:]
            xs1[pl.ds(4 * piece, 4)] = v.reshape(4, 64, RANK)

    def halves(total, compute, between):
        for n in (0, 2):
            compute(total.sibling_piece(n), total.sibling_piece(n + 1))
            if n == 0 and total is one:
                pl.semaphore_wait(barrier, len(peers))
            total.send_sibling(n)
            total.send_sibling(n + 1)
        between()
        compute(total.own_piece(0), total.own_piece(1))
        total.own_ready(0)
        total.own_ready(1)
        compute(total.own_piece(2), total.own_piece(3))
        total.own_ready(2)
        total.own_ready(3)

    halves(one, left_pieces, lambda: by_core(low.wait, high.wait))

    def merged_rows(i):
        r = pl.ds(i * PIECE, min(PIECE, TILE - i * PIECE))
        for n in range(8):
            k = pl.ds(n * PIECE, min(PIECE, TILE - n * PIECE))
            stored = e[r, k]
            ep[r, k] = stored
            merged_ref[r, k] = mm_t(at[r, :], gt[k, :]) + stored.astype(F32)

    for i in range(4):
        merged_rows(i)
    one.finish_scatter(lambda v: v)
    for i in range(4, 8):
        merged_rows(i)
    one.finish_spread()
    one.wait_sibling()

    for i in range(NCH):
        t_hi, t_lo = split(y1[pl.ds(2 * i, 2)].reshape(CH, RANK).T)
        lt[:RANK, pl.ds(i * CH, CH)] = t_hi
        lt[RANK:, pl.ds(i * CH, CH)] = t_lo
    tokens(at)

    def right_pieces(*pieces):
        done = [mm(lt[...], ep[:, place(i)]) + mm_t(pt[...], gt[place(i), :]) for i in pieces]
        for piece, v in zip(pieces, done):
            xs2[pl.ds(4 * piece, 4)] = (v[:RANK] + v[RANK:]).T.reshape(4, 64, RANK)

    halves(two, right_pieces, lambda: None)

    left = y1[...].reshape(PAD, RANK)
    row_i = lax.broadcasted_iota(jnp.int32, (RANK, RANK), 0)
    col_i = lax.broadcasted_iota(jnp.int32, (RANK, RANK), 1)
    gj[:, :RANK] = lax.dot_general(left, left, (((0,), (0,)), ((), ())), precision=PRECISE, preferred_element_type=F32)
    gj[:, RANK:] = jnp.where(row_i == col_i, 1.0, 0.0)

    def eliminate(first, count):
        def step(k, carry):
            row = gj[pl.ds(k, 1), :]
            whole = gj[...]
            pivot = jnp.sum(jnp.where(col_i[:1] == k, row[:, :RANK], 0.0), axis=1, keepdims=True)
            column = jnp.sum(jnp.where(col_i == k, whole[:, :RANK], 0.0), axis=1, keepdims=True)
            factor = jnp.where(row_i[:, :1] > k, column / pivot, 0.0)
            gj[...] = whole - factor * row
            return carry

        lax.fori_loop(first, first + count, step, 0)

    eliminate(0, RANK)
    diagonal = jnp.sum(jnp.where(row_i == col_i, gj[:, :RANK], 0.0), axis=1, keepdims=True)
    inverse = gj[:, RANK:] / jnp.sqrt(diagonal)
    scaled = inverse / 32.0
    squares = []

    def to_q(v):
        t = lax.dot_general(v, scaled, (((1,), (1,)), ((), ())), precision=PRECISE, preferred_element_type=F32)
        squares.append(t * t)
        return t

    two.finish_scatter(to_q)

    gone = []

    def exchange(i, ref, to):
        made = pltpu.make_async_remote_copy(
            src_ref=ref,
            dst_ref=ref,
            send_sem=n_send.at[i],
            recv_sem=n_recv.at[i],
            device_id=to,
            device_id_type=MESH,
        )
        made.start()
        gone.append(made)

    nt[y] = jnp.broadcast_to(jnp.sum(squares[0]), (8, RANK))
    for i, to in enumerate(tiles):
        exchange(i, nt.at[y], to)

    def ortho(first, count):
        for i in range(first, first + count):
            rows = min(CH, TILE - i * CH)
            o = lax.dot_general(
                y1[pl.ds(2 * i, 2)].reshape(CH, RANK), inverse, (((1,), (1,)), ((), ())), precision=PRECISE, preferred_element_type=F32
            )
            of[pl.ds(i * CH, CH), :] = o
            o_hi, o_lo = split(o[:rows])
            r = pl.ds(i * CH, rows)
            oo_ref[r, :RANK] = o_hi
            oo_ref[r, RANK : 2 * RANK] = o_hi
            oo_ref[r, 2 * RANK :] = o_lo

    ortho(0, NCH)
    for made in gone:
        made.wait_recv()
    nb[one.r] = (nt[0] + nt[1]) + (nt[2] + nt[3])
    for i, to in enumerate(chips):
        exchange(3 + i, nb.at[one.r], to)
    two.finish_spread()
    o_hi, o_lo = split(of[pl.ds(((z * 4 + x) * 2 + c) * OWNED, 64), :])
    own_ref[:, :RANK] = o_hi
    own_ref[:, RANK : 2 * RANK] = o_hi
    own_ref[:, 2 * RANK :] = o_lo
    one.wait_sends()
    for made in gone[3:]:
        made.wait_recv()
    norm = nb[0]
    for i in range(1, 16):
        norm = norm + nb[i]
    ns[c] = norm
    exchange(18, ns.at[c], one.sibling())
    two.wait_sibling()
    t = y2[...].reshape(PAD, RANK)[:TILE]
    t_hi, t_lo = split(t)
    qq_ref[:, :RANK] = t_hi
    qq_ref[:, RANK : 2 * RANK] = t_lo
    qq_ref[:, 2 * RANK :] = t_hi
    qn_ref[...] = t
    gone[-1].wait_recv()
    norm_ref[...] = ns[0] + ns[1]
    two.wait_sends()
    for made in gone:
        made.wait_send()


def compress(at, gt, error, q):
    any_spec = pl.BlockSpec(memory_space=pl.ANY)
    vmem = pl.BlockSpec(memory_space=pltpu.VMEM)
    parts = lambda n: pltpu.VMEM((n, 64, RANK), F32)
    sums = [parts(32), pltpu.VMEM((4, 4, 64, RANK), F32), parts(16), parts(32)]
    return pl.pallas_call(
        body,
        out_shape=(
            pltpu.VMEM((TILE, TILE), F32),
            pltpu.VMEM((TILE, 3 * RANK), BF16),
            pltpu.VMEM((TILE, 3 * RANK), BF16),
            pltpu.VMEM((TILE, RANK), F32),
            pltpu.VMEM((64, 3 * RANK), BF16),
            pltpu.VMEM((8, RANK), F32),
        ),
        in_specs=[any_spec] * 4,
        out_specs=(vmem,) * 6,
        scratch_shapes=[
            pltpu.VMEM((PAD, TOK), BF16),
            pltpu.VMEM((PAD, TOK), BF16),
            pltpu.VMEM((PAD, TILE), BF16),
            pltpu.VMEM((PAD, PAD), BF16),
            pltpu.VMEM((TILE, RANK), F32),
            pltpu.VMEM((TILE, 2 * RANK), BF16),
            pltpu.VMEM((2 * RANK, TOK), BF16),
            pltpu.VMEM((2 * RANK, PAD), BF16),
            pltpu.VMEM((RANK, 2 * RANK), F32),
            pltpu.VMEM((PAD, RANK), F32),
            pltpu.VMEM((4, 8, RANK), F32),
            pltpu.VMEM((16, 8, RANK), F32),
            pltpu.VMEM((2, 8, RANK), F32),
            *sums,
            *sums,
            pltpu.SemaphoreType.DMA((5,)),
            pltpu.SemaphoreType.DMA((2 * N_MSG,)),
            pltpu.SemaphoreType.DMA((2 * N_MSG,)),
            pltpu.SemaphoreType.DMA((19,)),
            pltpu.SemaphoreType.DMA((19,)),
        ],
        compiler_params=pltpu.CompilerParams(
            collective_id=0, has_side_effects=True, vmem_limit_bytes=42 * 1024 * 1024
        ),
        name="compress",
    )(at, gt, error, q)


def finish(merged, oo, qq, qn, own, norm, momentum):
    rows = TILE // 4

    def block(m_ref, o_ref, q_ref, n_ref, own_ref, norm_ref, mom_ref, out_ref, next_ref, qn_ref):
        i = pl.program_id(0)
        at = pl.ds(pl.multiple_of(i * rows, 16), rows)
        columns = [pl.ds(n * PIECE, min(PIECE, TILE - n * PIECE)) for n in range(8)]
        for k in columns:
            out_ref[:, k] = (m_ref[at, k] - mm_t(o_ref[at, :], q_ref[k, :])).astype(BF16)
        qn_ref[...] = n_ref[at, :]

        @pl.when(i == 0)
        def _():
            rms = jnp.sqrt(norm_ref[:1, :1] / (D * D))
            scale = 0.1 / (rms + 1e-6)
            for k in columns:
                next_ref[:, k] = 0.9 * mom_ref[:, k] + scale * mm_t(own_ref[...], q_ref[k, :])[:OWNED]

    vmem = pl.BlockSpec(memory_space=pltpu.VMEM)
    held = [pltpu.with_memory_space_constraint(v, pltpu.VMEM) for v in (merged, oo, qq, qn, own, norm)]
    whole = pl.BlockSpec((OWNED, TILE), lambda i: (0, 0))
    return pl.pallas_call(
        block,
        grid=(4,),
        out_shape=(
            jax.ShapeDtypeStruct((TILE, TILE), BF16),
            jax.ShapeDtypeStruct((OWNED, TILE), F32),
            jax.ShapeDtypeStruct((TILE, RANK), F32),
        ),
        in_specs=[vmem] * 6 + [whole],
        out_specs=(
            pl.BlockSpec((rows, TILE), lambda i: (i, 0)),
            whole,
            pl.BlockSpec((rows, RANK), lambda i: (i, 0)),
        ),
        compiler_params=pltpu.CompilerParams(vmem_limit_bytes=16 * 1024 * 1024),
        name="finish",
    )(*held, momentum)


def per_device(acts, grads, error, momentum, q_start):
    at, gt = acts[:, 0, :].T, grads[:, 0, :].T
    made = compress(at, gt, error[0, 0], q_start[0])
    error_next, momentum_next, q_tile = finish(*made, momentum[0])
    return (error_next[None, None], momentum_next[None], q_tile[None])


def solution(mesh):
    split_mesh = Mesh(mesh.devices.reshape(4, 4, 2, mesh.shape["mp"]), (*DP, "mp"))
    in_specs = (
        P(DP, "mp", None),
        P(DP, "mp", None),
        P(DP, "mp", None, None),
        P("mp", DP, None),
        P("mp", None, None),
    )
    out_specs = (P(DP, "mp", None, None), P("mp", DP, None), P("mp", None, None))
    return jax.shard_map(
        per_device, mesh=split_mesh, in_specs=in_specs, out_specs=out_specs, check_vma=False
    )
```

```python
import jax
import jax.numpy as jnp
from jax import lax
from jax.experimental import pallas as pl
from jax.experimental.pallas import tpu as pltpu
from jax.sharding import Mesh
from jax.sharding import PartitionSpec as P

D = 3968
DP = ("dp_0", "dp_1", "dp_2")
MESH = pl.DeviceIdType.MESH
TILE = 1984
PAD = 2048
RANK = 128
TOK = 768
CH = 128
NCH = 16
PIECE = 256
F32 = jnp.float32
BF16 = jnp.bfloat16
PRECISE = lax.Precision.HIGHEST
ORDER = (2, 1, 3, 0)
CHIPS = [(z, x) for z in ORDER for x in ORDER if z or x]
N_MSG = 35
OWNED = 62


def mm(a, b):
    return jnp.dot(a, b, preferred_element_type=F32)


def mm_t(a, b):
    return lax.dot_general(a, b, (((1,), (1,)), ((), ())), preferred_element_type=F32)


def split(v):
    hi = v.astype(BF16)
    return hi, (v - hi.astype(F32)).astype(BF16)


class Sum:
    def __init__(self, pos, bufs, sems, base):
        self.z, self.x, self.c, self.y = pos
        self.xs, self.sib, self.slots, self.out = bufs
        self.send, self.recv = sems
        self.base = base
        self.started = []
        self.r = 4 * self.z + self.x
        self.from_sibling, self.scattered, self.spread = {}, [], []

    def chip(self, dz, dx):
        return lax.rem(self.z + dz, 4), lax.rem(self.x + dx, 4)

    def sibling(self):
        return (self.z, self.x, 1 - self.c, self.y)

    def copy(self, i, src, dst, to):
        made = pltpu.make_async_remote_copy(
            src_ref=src,
            dst_ref=dst,
            send_sem=self.send.at[self.base + i],
            recv_sem=self.recv.at[self.base + i],
            device_id=to,
            device_id_type=MESH,
        )
        made.start()
        self.started.append(made)
        return made

    def sibling_piece(self, n):
        return 4 * (1 - self.c) + lax.rem(self.z + ORDER[n], 4)

    def own_piece(self, n):
        return 4 * self.c + lax.rem(self.z + ORDER[n], 4)

    def send_sibling(self, n):
        i = 4 * self.sibling_piece(n)
        self.from_sibling[n] = self.copy(n, self.xs.at[pl.ds(i, 4)], self.sib.at[n], self.sibling())

    def own_ready(self, n):
        i = pl.ds(4 * self.own_piece(n), 4)
        self.from_sibling[n].wait_recv()
        self.xs[i] = self.xs[i] + self.sib[n]
        for dx in ORDER:
            if not (ORDER[n] or dx):
                continue
            z, x = self.chip(ORDER[n], dx)
            made = self.copy(
                4 + len(self.scattered),
                self.xs.at[16 * self.c + 4 * z + x],
                self.slots.at[self.r],
                (z, x, self.c, self.y),
            )
            self.scattered.append(made)

    def finish_scatter(self, change):
        mine = 16 * self.c + self.r
        self.slots[self.r] = self.xs[mine]
        for made in self.scattered:
            made.wait_recv()
        total = self.slots[0]
        for i in range(1, 16):
            total = total + self.slots[i]
        self.out[mine] = change(total)
        part = self.out.at[mine]
        for n, (dz, dx) in enumerate(CHIPS):
            self.spread.append(self.copy(19 + n, part, part, (*self.chip(dz, dx), self.c, self.y)))

    def finish_spread(self):
        for made in self.spread:
            made.wait_recv()
        part = self.out.at[pl.ds(16 * self.c, 16)]
        self.to_sibling = self.copy(34, part, part, self.sibling())

    def wait_sibling(self):
        self.to_sibling.wait_recv()

    def wait_sends(self):
        for made in self.started:
            made.wait_send()


def body(
    at_hbm, gt_hbm, e_hbm, q_hbm,
    merged_ref, oo_ref, qq_ref, qn_ref, own_ref, norm_ref,
    at, gt, e, ep, q, qs, pt, lt, gj, of, nt, nb, ns,
    xs1, sib1, slots1, y1,
    xs2, sib2, slots2, y2,
    in_sem, send, recv, n_send, n_recv,
):
    z, x, c, y = (lax.axis_index(a) for a in (*DP, "mp"))
    pos = (z, x, c, y)
    half = PAD // 2
    loads = [
        pltpu.make_async_copy(q_hbm, q, in_sem.at[0]),
        pltpu.make_async_copy(gt_hbm, gt.at[pl.ds(0, TILE)], in_sem.at[1]),
        pltpu.make_async_copy(at_hbm, at.at[pl.ds(0, TILE)], in_sem.at[2]),
    ]
    low = pltpu.make_async_copy(e_hbm.at[pl.ds(0, half)], e.at[pl.ds(0, half)], in_sem.at[3])
    high = pltpu.make_async_copy(e_hbm.at[pl.ds(half, TILE - half)], e.at[pl.ds(half, TILE - half)], in_sem.at[4])
    for load in loads:
        load.start()

    def by_core(first, second):
        pl.when(c == 0)(first)
        pl.when(c == 1)(second)

    by_core(high.start, low.start)
    by_core(low.start, high.start)
    one = Sum(pos, (xs1, sib1, slots1, y1), (send, recv), 0)
    two = Sum(pos, (xs2, sib2, slots2, y2), (send, recv), N_MSG)

    tiles = [(z, x, c, lax.rem(y + d, 4)) for d in (1, 2, 3)]
    chips = [(*one.chip(dz, dx), c, y) for dz, dx in CHIPS]
    barrier = pltpu.get_barrier_semaphore()
    peers = [one.sibling(), *tiles, *chips]
    for peer in peers:
        pl.semaphore_signal(barrier, inc=1, device_id=peer, device_id_type=MESH)

    for ref in (at, gt, e, ep):
        ref[pl.ds(TILE, PAD - TILE), :] = jnp.zeros((PAD - TILE, ref.shape[1]), BF16)
    ep[:, pl.ds(TILE, PAD - TILE)] = jnp.zeros((PAD, PAD - TILE), BF16)

    loads[0].wait()
    hi, lo = split(q[...])
    qs[:, :RANK] = hi
    qs[:, RANK:] = lo
    for i in range(NCH):
        rows = min(CH, TILE - i * CH)
        t_hi, t_lo = split(q[pl.ds(i * CH, rows), :].T)
        lt[:RANK, pl.ds(i * CH, rows)] = t_hi
        lt[RANK:, pl.ds(i * CH, rows)] = t_lo
    lt[:, pl.ds(TILE, PAD - TILE)] = jnp.zeros((2 * RANK, PAD - TILE), BF16)
    loads[1].wait()

    def tokens(ref):
        for n in range(TOK // PIECE):
            cols = pl.ds(n * PIECE, PIECE)
            v = mm(lt[...], ref[:, cols])
            v_hi, v_lo = split(v[:RANK] + v[RANK:])
            pt[:RANK, cols] = v_hi
            pt[RANK:, cols] = v_lo

    tokens(gt)
    loads[2].wait()
    by_core(high.wait, low.wait)

    def place(piece):
        return pl.ds(pl.multiple_of(piece * PIECE, PIECE), PIECE)

    def left_pieces(*pieces):
        done = [mm(e[place(i), :], qs[...]) + mm_t(at[place(i), :], pt[...]) for i in pieces]
        for piece, v in zip(pieces, done):
            v = v[:, :RANK] + v[:, RANK:]
            xs1[pl.ds(4 * piece, 4)] = v.reshape(4, 64, RANK)

    def halves(total, compute, between):
        for n in (0, 2):
            compute(total.sibling_piece(n), total.sibling_piece(n + 1))
            if n == 0 and total is one:
                pl.semaphore_wait(barrier, len(peers))
            total.send_sibling(n)
            total.send_sibling(n + 1)
        between()
        compute(total.own_piece(0), total.own_piece(1))
        total.own_ready(0)
        total.own_ready(1)
        compute(total.own_piece(2), total.own_piece(3))
        total.own_ready(2)
        total.own_ready(3)

    halves(one, left_pieces, lambda: by_core(low.wait, high.wait))

    def merged_rows(i):
        r = pl.ds(i * PIECE, min(PIECE, TILE - i * PIECE))
        for n in range(8):
            k = pl.ds(n * PIECE, min(PIECE, TILE - n * PIECE))
            stored = e[r, k]
            ep[r, k] = stored
            merged_ref[r, k] = mm_t(at[r, :], gt[k, :]) + stored.astype(F32)

    for i in range(4):
        merged_rows(i)
    one.finish_scatter(lambda v: v)
    for i in range(4, 8):
        merged_rows(i)
    one.finish_spread()
    one.wait_sibling()

    for i in range(NCH):
        t_hi, t_lo = split(y1[pl.ds(2 * i, 2)].reshape(CH, RANK).T)
        lt[:RANK, pl.ds(i * CH, CH)] = t_hi
        lt[RANK:, pl.ds(i * CH, CH)] = t_lo
    tokens(at)

    def right_pieces(*pieces):
        done = [mm(lt[...], ep[:, place(i)]) + mm_t(pt[...], gt[place(i), :]) for i in pieces]
        for piece, v in zip(pieces, done):
            xs2[pl.ds(4 * piece, 4)] = (v[:RANK] + v[RANK:]).T.reshape(4, 64, RANK)

    halves(two, right_pieces, lambda: None)

    left = y1[...].reshape(PAD, RANK)
    row_i = lax.broadcasted_iota(jnp.int32, (RANK, RANK), 0)
    col_i = lax.broadcasted_iota(jnp.int32, (RANK, RANK), 1)
    gj[:, :RANK] = lax.dot_general(left, left, (((0,), (0,)), ((), ())), precision=PRECISE, preferred_element_type=F32)
    gj[:, RANK:] = jnp.where(row_i == col_i, 1.0, 0.0)

    def eliminate(first, count, width):
        live = pl.ds(first, RANK - first)
        row_at = lax.broadcasted_iota(jnp.int32, (RANK - first, 1), 0) + first
        lane = col_i[:1]

        def pick(v, k):
            return jnp.sum(jnp.where(lane == k, v[:, :RANK], 0.0), axis=1, keepdims=True)

        def step(n, carry):
            k = first + width * n
            whole = gj[live, :]
            rows = [gj[pl.ds(k + i, 1), :] for i in range(width)]
            columns = [pick(whole, k + i) for i in range(width)]
            block = [[pick(rows[i], k + j) for j in range(width)] for i in range(width)]
            for i in range(width):
                inverse = 1.0 / block[i][i]
                factor = jnp.where(row_at > k + i, columns[i] * inverse, 0.0)
                for j in range(i + 1, width):
                    f = block[j][i] * inverse
                    columns[j] = columns[j] - factor * block[i][j]
                    rows[j] = rows[j] - f * rows[i]
                    for m in range(i + 1, width):
                        block[j][m] = block[j][m] - f * block[i][m]
                whole = whole - factor * rows[i]
            gj[live, :] = whole
            return carry

        lax.fori_loop(0, count // width, step, 0)

    for first in range(0, RANK, RANK // 4):
        eliminate(first, RANK // 4, 4)
    diagonal = jnp.sum(jnp.where(row_i == col_i, gj[:, :RANK], 0.0), axis=1, keepdims=True)
    inverse = gj[:, RANK:] / jnp.sqrt(diagonal)
    scaled = inverse / 32.0
    squares = []

    def to_q(v):
        t = lax.dot_general(v, scaled, (((1,), (1,)), ((), ())), precision=PRECISE, preferred_element_type=F32)
        squares.append(t * t)
        return t

    two.finish_scatter(to_q)

    gone = []

    def exchange(i, ref, to):
        made = pltpu.make_async_remote_copy(
            src_ref=ref,
            dst_ref=ref,
            send_sem=n_send.at[i],
            recv_sem=n_recv.at[i],
            device_id=to,
            device_id_type=MESH,
        )
        made.start()
        gone.append(made)

    nt[y] = jnp.broadcast_to(jnp.sum(squares[0]), (8, RANK))
    for i, to in enumerate(tiles):
        exchange(i, nt.at[y], to)

    def ortho(first, count):
        for i in range(first, first + count):
            rows = min(CH, TILE - i * CH)
            o = lax.dot_general(
                y1[pl.ds(2 * i, 2)].reshape(CH, RANK), inverse, (((1,), (1,)), ((), ())), precision=PRECISE, preferred_element_type=F32
            )
            of[pl.ds(i * CH, CH), :] = o
            o_hi, o_lo = split(o[:rows])
            r = pl.ds(i * CH, rows)
            oo_ref[r, :RANK] = o_hi
            oo_ref[r, RANK : 2 * RANK] = o_hi
            oo_ref[r, 2 * RANK :] = o_lo

    ortho(0, NCH)
    for made in gone:
        made.wait_recv()
    nb[one.r] = (nt[0] + nt[1]) + (nt[2] + nt[3])
    for i, to in enumerate(chips):
        exchange(3 + i, nb.at[one.r], to)
    two.finish_spread()
    o_hi, o_lo = split(of[pl.ds(((z * 4 + x) * 2 + c) * OWNED, 64), :])
    own_ref[:, :RANK] = o_hi
    own_ref[:, RANK : 2 * RANK] = o_hi
    own_ref[:, 2 * RANK :] = o_lo
    one.wait_sends()
    for made in gone[3:]:
        made.wait_recv()
    norm = nb[0]
    for i in range(1, 16):
        norm = norm + nb[i]
    ns[c] = norm
    exchange(18, ns.at[c], one.sibling())
    two.wait_sibling()
    t = y2[...].reshape(PAD, RANK)[:TILE]
    t_hi, t_lo = split(t)
    qq_ref[:, :RANK] = t_hi
    qq_ref[:, RANK : 2 * RANK] = t_lo
    qq_ref[:, 2 * RANK :] = t_hi
    qn_ref[...] = t
    gone[-1].wait_recv()
    norm_ref[...] = ns[0] + ns[1]
    two.wait_sends()
    for made in gone:
        made.wait_send()


def compress(at, gt, error, q):
    any_spec = pl.BlockSpec(memory_space=pl.ANY)
    vmem = pl.BlockSpec(memory_space=pltpu.VMEM)
    parts = lambda n: pltpu.VMEM((n, 64, RANK), F32)
    sums = [parts(32), pltpu.VMEM((4, 4, 64, RANK), F32), parts(16), parts(32)]
    return pl.pallas_call(
        body,
        out_shape=(
            pltpu.VMEM((TILE, TILE), F32),
            pltpu.VMEM((TILE, 3 * RANK), BF16),
            pltpu.VMEM((TILE, 3 * RANK), BF16),
            pltpu.VMEM((TILE, RANK), F32),
            pltpu.VMEM((64, 3 * RANK), BF16),
            pltpu.VMEM((8, RANK), F32),
        ),
        in_specs=[any_spec] * 4,
        out_specs=(vmem,) * 6,
        scratch_shapes=[
            pltpu.VMEM((PAD, TOK), BF16),
            pltpu.VMEM((PAD, TOK), BF16),
            pltpu.VMEM((PAD, TILE), BF16),
            pltpu.VMEM((PAD, PAD), BF16),
            pltpu.VMEM((TILE, RANK), F32),
            pltpu.VMEM((TILE, 2 * RANK), BF16),
            pltpu.VMEM((2 * RANK, TOK), BF16),
            pltpu.VMEM((2 * RANK, PAD), BF16),
            pltpu.VMEM((RANK, 2 * RANK), F32),
            pltpu.VMEM((PAD, RANK), F32),
            pltpu.VMEM((4, 8, RANK), F32),
            pltpu.VMEM((16, 8, RANK), F32),
            pltpu.VMEM((2, 8, RANK), F32),
            *sums,
            *sums,
            pltpu.SemaphoreType.DMA((5,)),
            pltpu.SemaphoreType.DMA((2 * N_MSG,)),
            pltpu.SemaphoreType.DMA((2 * N_MSG,)),
            pltpu.SemaphoreType.DMA((19,)),
            pltpu.SemaphoreType.DMA((19,)),
        ],
        compiler_params=pltpu.CompilerParams(
            collective_id=0, has_side_effects=True, vmem_limit_bytes=42 * 1024 * 1024
        ),
        name="compress",
    )(at, gt, error, q)


def finish(merged, oo, qq, qn, own, norm, momentum):
    rows = TILE // 4

    def block(m_ref, o_ref, q_ref, n_ref, own_ref, norm_ref, mom_ref, out_ref, next_ref, qn_ref):
        i = pl.program_id(0)
        at = pl.ds(pl.multiple_of(i * rows, 16), rows)
        columns = [pl.ds(n * PIECE, min(PIECE, TILE - n * PIECE)) for n in range(8)]
        for k in columns:
            out_ref[:, k] = (m_ref[at, k] - mm_t(o_ref[at, :], q_ref[k, :])).astype(BF16)
        qn_ref[...] = n_ref[at, :]

        @pl.when(i == 0)
        def _():
            rms = jnp.sqrt(norm_ref[:1, :1] / (D * D))
            scale = 0.1 / (rms + 1e-6)
            for k in columns:
                next_ref[:, k] = 0.9 * mom_ref[:, k] + scale * mm_t(own_ref[...], q_ref[k, :])[:OWNED]

    vmem = pl.BlockSpec(memory_space=pltpu.VMEM)
    held = [pltpu.with_memory_space_constraint(v, pltpu.VMEM) for v in (merged, oo, qq, qn, own, norm)]
    whole = pl.BlockSpec((OWNED, TILE), lambda i: (0, 0))
    return pl.pallas_call(
        block,
        grid=(4,),
        out_shape=(
            jax.ShapeDtypeStruct((TILE, TILE), BF16),
            jax.ShapeDtypeStruct((OWNED, TILE), F32),
            jax.ShapeDtypeStruct((TILE, RANK), F32),
        ),
        in_specs=[vmem] * 6 + [whole],
        out_specs=(
            pl.BlockSpec((rows, TILE), lambda i: (i, 0)),
            whole,
            pl.BlockSpec((rows, RANK), lambda i: (i, 0)),
        ),
        compiler_params=pltpu.CompilerParams(vmem_limit_bytes=16 * 1024 * 1024),
        name="finish",
    )(*held, momentum)


def per_device(acts, grads, error, momentum, q_start):
    at, gt = acts[:, 0, :].T, grads[:, 0, :].T
    made = compress(at, gt, error[0, 0], q_start[0])
    error_next, momentum_next, q_tile = finish(*made, momentum[0])
    return (error_next[None, None], momentum_next[None], q_tile[None])


def solution(mesh):
    split_mesh = Mesh(mesh.devices.reshape(4, 4, 2, mesh.shape["mp"]), (*DP, "mp"))
    in_specs = (
        P(DP, "mp", None),
        P(DP, "mp", None),
        P(DP, "mp", None, None),
        P("mp", DP, None),
        P("mp", None, None),
    )
    out_specs = (P(DP, "mp", None, None), P("mp", DP, None), P("mp", None, None))
    return jax.shard_map(
        per_device, mesh=split_mesh, in_specs=in_specs, out_specs=out_specs, check_vma=False
    )
```

```python
import jax
import jax.numpy as jnp
from jax import lax
from jax.experimental import pallas as pl
from jax.experimental.pallas import tpu as pltpu
from jax.sharding import Mesh
from jax.sharding import PartitionSpec as P

D = 3968
DP = ("dp_0", "dp_1", "dp_2")
MESH = pl.DeviceIdType.MESH
TILE = 1984
PAD = 2048
RANK = 128
TOK = 768
CH = 128
NCH = 16
PIECE = 256
F32 = jnp.float32
BF16 = jnp.bfloat16
PRECISE = lax.Precision.HIGHEST
ORDER = (2, 1, 3, 0)
CHIPS = [(z, x) for z in ORDER for x in ORDER if z or x]
N_MSG = 35
OWNED = 62


def mm(a, b):
    return jnp.dot(a, b, preferred_element_type=F32)


def mm_t(a, b):
    return lax.dot_general(a, b, (((1,), (1,)), ((), ())), preferred_element_type=F32)


def split(v):
    hi = v.astype(BF16)
    return hi, (v - hi.astype(F32)).astype(BF16)


class Sum:
    def __init__(self, pos, bufs, sems, base):
        self.z, self.x, self.c, self.y = pos
        self.xs, self.sib, self.slots, self.out = bufs
        self.send, self.recv = sems
        self.base = base
        self.started = []
        self.r = 4 * self.z + self.x
        self.from_sibling, self.scattered, self.spread = {}, [], []

    def chip(self, dz, dx):
        return lax.rem(self.z + dz, 4), lax.rem(self.x + dx, 4)

    def sibling(self):
        return (self.z, self.x, 1 - self.c, self.y)

    def copy(self, i, src, dst, to):
        made = pltpu.make_async_remote_copy(
            src_ref=src,
            dst_ref=dst,
            send_sem=self.send.at[self.base + i],
            recv_sem=self.recv.at[self.base + i],
            device_id=to,
            device_id_type=MESH,
        )
        made.start()
        self.started.append(made)
        return made

    def sibling_piece(self, n):
        return 4 * (1 - self.c) + lax.rem(self.z + ORDER[n], 4)

    def own_piece(self, n):
        return 4 * self.c + lax.rem(self.z + ORDER[n], 4)

    def send_sibling(self, n):
        i = 4 * self.sibling_piece(n)
        self.from_sibling[n] = self.copy(n, self.xs.at[pl.ds(i, 4)], self.sib.at[n], self.sibling())

    def own_ready(self, n):
        i = pl.ds(4 * self.own_piece(n), 4)
        self.from_sibling[n].wait_recv()
        self.xs[i] = self.xs[i] + self.sib[n]
        for dx in ORDER:
            if not (ORDER[n] or dx):
                continue
            z, x = self.chip(ORDER[n], dx)
            made = self.copy(
                4 + len(self.scattered),
                self.xs.at[16 * self.c + 4 * z + x],
                self.slots.at[self.r],
                (z, x, self.c, self.y),
            )
            self.scattered.append(made)

    def finish_scatter(self, change):
        mine = 16 * self.c + self.r
        self.slots[self.r] = self.xs[mine]
        for made in self.scattered:
            made.wait_recv()
        total = self.slots[0]
        for i in range(1, 16):
            total = total + self.slots[i]
        self.out[mine] = change(total)
        part = self.out.at[mine]
        for n, (dz, dx) in enumerate(CHIPS):
            self.spread.append(self.copy(19 + n, part, part, (*self.chip(dz, dx), self.c, self.y)))

    def finish_spread(self):
        for made in self.spread:
            made.wait_recv()
        part = self.out.at[pl.ds(16 * self.c, 16)]
        self.to_sibling = self.copy(34, part, part, self.sibling())

    def wait_sibling(self):
        self.to_sibling.wait_recv()

    def wait_sends(self):
        for made in self.started:
            made.wait_send()


def body(
    at_hbm, gt_hbm, e_hbm, q_hbm, mom_hbm,
    merged_ref, oo_ref, qq_ref, qn_ref, own_ref, norm_ref, mom_ref,
    at, gt, e, ep, q, qs, pt, lt, gj, of, nt, nb, ns, mom,
    xs1, sib1, slots1, y1,
    xs2, sib2, slots2, y2,
    in_sem, send, recv, n_send, n_recv,
):
    z, x, c, y = (lax.axis_index(a) for a in (*DP, "mp"))
    pos = (z, x, c, y)
    half = PAD // 2
    loads = [
        pltpu.make_async_copy(q_hbm, q, in_sem.at[0]),
        pltpu.make_async_copy(gt_hbm, gt.at[pl.ds(0, TILE)], in_sem.at[1]),
        pltpu.make_async_copy(at_hbm, at.at[pl.ds(0, TILE)], in_sem.at[2]),
    ]
    low = pltpu.make_async_copy(e_hbm.at[pl.ds(0, half)], e.at[pl.ds(0, half)], in_sem.at[3])
    high = pltpu.make_async_copy(e_hbm.at[pl.ds(half, TILE - half)], e.at[pl.ds(half, TILE - half)], in_sem.at[4])
    for load in loads:
        load.start()

    def by_core(first, second):
        pl.when(c == 0)(first)
        pl.when(c == 1)(second)

    by_core(high.start, low.start)
    by_core(low.start, high.start)
    last = pltpu.make_async_copy(mom_hbm, mom, in_sem.at[5])
    last.start()
    one = Sum(pos, (xs1, sib1, slots1, y1), (send, recv), 0)
    two = Sum(pos, (xs2, sib2, slots2, y2), (send, recv), N_MSG)

    tiles = [(z, x, c, lax.rem(y + d, 4)) for d in (1, 2, 3)]
    chips = [(*one.chip(dz, dx), c, y) for dz, dx in CHIPS]
    barrier = pltpu.get_barrier_semaphore()
    peers = [one.sibling(), *tiles, *chips]
    for peer in peers:
        pl.semaphore_signal(barrier, inc=1, device_id=peer, device_id_type=MESH)

    for ref in (at, gt, e, ep):
        ref[pl.ds(TILE, PAD - TILE), :] = jnp.zeros((PAD - TILE, ref.shape[1]), BF16)
    ep[:, pl.ds(TILE, PAD - TILE)] = jnp.zeros((PAD, PAD - TILE), BF16)

    loads[0].wait()
    hi, lo = split(q[...])
    qs[:, :RANK] = hi
    qs[:, RANK:] = lo
    for i in range(NCH):
        rows = min(CH, TILE - i * CH)
        t_hi, t_lo = split(q[pl.ds(i * CH, rows), :].T)
        lt[:RANK, pl.ds(i * CH, rows)] = t_hi
        lt[RANK:, pl.ds(i * CH, rows)] = t_lo
    lt[:, pl.ds(TILE, PAD - TILE)] = jnp.zeros((2 * RANK, PAD - TILE), BF16)
    loads[1].wait()

    def tokens(ref):
        for n in range(TOK // PIECE):
            cols = pl.ds(n * PIECE, PIECE)
            v = mm(lt[...], ref[:, cols])
            v_hi, v_lo = split(v[:RANK] + v[RANK:])
            pt[:RANK, cols] = v_hi
            pt[RANK:, cols] = v_lo

    tokens(gt)
    loads[2].wait()
    by_core(high.wait, low.wait)

    def place(piece):
        return pl.ds(pl.multiple_of(piece * PIECE, PIECE), PIECE)

    def left_pieces(*pieces):
        done = [mm(e[place(i), :], qs[...]) + mm_t(at[place(i), :], pt[...]) for i in pieces]
        for piece, v in zip(pieces, done):
            v = v[:, :RANK] + v[:, RANK:]
            xs1[pl.ds(4 * piece, 4)] = v.reshape(4, 64, RANK)

    def halves(total, compute, between):
        for n in (0, 2):
            compute(total.sibling_piece(n), total.sibling_piece(n + 1))
            if n == 0 and total is one:
                pl.semaphore_wait(barrier, len(peers))
            total.send_sibling(n)
            total.send_sibling(n + 1)
        between()
        compute(total.own_piece(0), total.own_piece(1))
        total.own_ready(0)
        total.own_ready(1)
        compute(total.own_piece(2), total.own_piece(3))
        total.own_ready(2)
        total.own_ready(3)

    halves(one, left_pieces, lambda: by_core(low.wait, high.wait))

    def merged_rows(i):
        r = pl.ds(i * PIECE, min(PIECE, TILE - i * PIECE))
        for n in range(8):
            k = pl.ds(n * PIECE, min(PIECE, TILE - n * PIECE))
            stored = e[r, k]
            ep[r, k] = stored
            merged_ref[r, k] = mm_t(at[r, :], gt[k, :]) + stored.astype(F32)

    for i in range(4):
        merged_rows(i)
    one.finish_scatter(lambda v: v)
    last.wait()
    mom_ref[...] = mom[:, 0, :]
    for i in range(4, 8):
        merged_rows(i)
    one.finish_spread()
    one.wait_sibling()

    for i in range(NCH):
        t_hi, t_lo = split(y1[pl.ds(2 * i, 2)].reshape(CH, RANK).T)
        lt[:RANK, pl.ds(i * CH, CH)] = t_hi
        lt[RANK:, pl.ds(i * CH, CH)] = t_lo
    tokens(at)

    def right_pieces(*pieces):
        done = [mm(lt[...], ep[:, place(i)]) + mm_t(pt[...], gt[place(i), :]) for i in pieces]
        for piece, v in zip(pieces, done):
            xs2[pl.ds(4 * piece, 4)] = (v[:RANK] + v[RANK:]).T.reshape(4, 64, RANK)

    halves(two, right_pieces, lambda: None)

    left = y1[...].reshape(PAD, RANK)
    row_i = lax.broadcasted_iota(jnp.int32, (RANK, RANK), 0)
    col_i = lax.broadcasted_iota(jnp.int32, (RANK, RANK), 1)
    gj[:, :RANK] = lax.dot_general(left, left, (((0,), (0,)), ((), ())), precision=PRECISE, preferred_element_type=F32)
    gj[:, RANK:] = jnp.where(row_i == col_i, 1.0, 0.0)

    def eliminate(first, count, width):
        live = pl.ds(first, RANK - first)
        row_at = lax.broadcasted_iota(jnp.int32, (RANK - first, 1), 0) + first
        lane = col_i[:1]

        def pick(v, k):
            return jnp.sum(jnp.where(lane == k, v[:, :RANK], 0.0), axis=1, keepdims=True)

        def step(n, carry):
            k = first + width * n
            whole = gj[live, :]
            rows = [gj[pl.ds(k + i, 1), :] for i in range(width)]
            columns = [pick(whole, k + i) for i in range(width)]
            block = [[pick(rows[i], k + j) for j in range(width)] for i in range(width)]
            for i in range(width):
                inverse = 1.0 / block[i][i]
                factor = jnp.where(row_at > k + i, columns[i] * inverse, 0.0)
                for j in range(i + 1, width):
                    f = block[j][i] * inverse
                    columns[j] = columns[j] - factor * block[i][j]
                    rows[j] = rows[j] - f * rows[i]
                    for m in range(i + 1, width):
                        block[j][m] = block[j][m] - f * block[i][m]
                whole = whole - factor * rows[i]
            gj[live, :] = whole
            return carry

        lax.fori_loop(0, count // width, step, 0)

    for first in range(0, RANK, RANK // 4):
        eliminate(first, RANK // 4, 4)
    diagonal = jnp.sum(jnp.where(row_i == col_i, gj[:, :RANK], 0.0), axis=1, keepdims=True)
    inverse = gj[:, RANK:] / jnp.sqrt(diagonal)
    scaled = inverse / 32.0
    squares = []

    def to_q(v):
        t = lax.dot_general(v, scaled, (((1,), (1,)), ((), ())), precision=PRECISE, preferred_element_type=F32)
        squares.append(t * t)
        return t

    two.finish_scatter(to_q)

    gone = []

    def exchange(i, ref, to):
        made = pltpu.make_async_remote_copy(
            src_ref=ref,
            dst_ref=ref,
            send_sem=n_send.at[i],
            recv_sem=n_recv.at[i],
            device_id=to,
            device_id_type=MESH,
        )
        made.start()
        gone.append(made)

    nt[y] = jnp.broadcast_to(jnp.sum(squares[0]), (8, RANK))
    for i, to in enumerate(tiles):
        exchange(i, nt.at[y], to)

    def ortho(first, count):
        for i in range(first, first + count):
            rows = min(CH, TILE - i * CH)
            o = lax.dot_general(
                y1[pl.ds(2 * i, 2)].reshape(CH, RANK), inverse, (((1,), (1,)), ((), ())), precision=PRECISE, preferred_element_type=F32
            )
            of[pl.ds(i * CH, CH), :] = o
            o_hi, o_lo = split(o[:rows])
            r = pl.ds(i * CH, rows)
            oo_ref[r, :RANK] = o_hi
            oo_ref[r, RANK : 2 * RANK] = o_hi
            oo_ref[r, 2 * RANK :] = o_lo

    ortho(0, NCH)
    for made in gone:
        made.wait_recv()
    nb[one.r] = (nt[0] + nt[1]) + (nt[2] + nt[3])
    for i, to in enumerate(chips):
        exchange(3 + i, nb.at[one.r], to)
    two.finish_spread()
    o_hi, o_lo = split(of[pl.ds(((z * 4 + x) * 2 + c) * OWNED, 64), :])
    own_ref[:, :RANK] = o_hi
    own_ref[:, RANK : 2 * RANK] = o_hi
    own_ref[:, 2 * RANK :] = o_lo
    one.wait_sends()
    for made in gone[3:]:
        made.wait_recv()
    norm = nb[0]
    for i in range(1, 16):
        norm = norm + nb[i]
    ns[c] = norm
    exchange(18, ns.at[c], one.sibling())
    two.wait_sibling()
    t = y2[...].reshape(PAD, RANK)[:TILE]
    t_hi, t_lo = split(t)
    qq_ref[:, :RANK] = t_hi
    qq_ref[:, RANK : 2 * RANK] = t_lo
    qq_ref[:, 2 * RANK :] = t_hi
    qn_ref[...] = t
    gone[-1].wait_recv()
    norm_ref[...] = ns[0] + ns[1]
    two.wait_sends()
    for made in gone:
        made.wait_send()


def compress(at, gt, error, q, momentum):
    any_spec = pl.BlockSpec(memory_space=pl.ANY)
    vmem = pl.BlockSpec(memory_space=pltpu.VMEM)
    parts = lambda n: pltpu.VMEM((n, 64, RANK), F32)
    sums = [parts(32), pltpu.VMEM((4, 4, 64, RANK), F32), parts(16), parts(32)]
    return pl.pallas_call(
        body,
        out_shape=(
            pltpu.VMEM((TILE, TILE), F32),
            pltpu.VMEM((TILE, 3 * RANK), BF16),
            pltpu.VMEM((TILE, 3 * RANK), BF16),
            pltpu.VMEM((TILE, RANK), F32),
            pltpu.VMEM((64, 3 * RANK), BF16),
            pltpu.VMEM((8, RANK), F32),
            pltpu.VMEM((OWNED, TILE), F32),
        ),
        in_specs=[any_spec] * 5,
        out_specs=(vmem,) * 7,
        scratch_shapes=[
            pltpu.VMEM((PAD, TOK), BF16),
            pltpu.VMEM((PAD, TOK), BF16),
            pltpu.VMEM((PAD, TILE), BF16),
            pltpu.VMEM((PAD, PAD), BF16),
            pltpu.VMEM((TILE, RANK), F32),
            pltpu.VMEM((TILE, 2 * RANK), BF16),
            pltpu.VMEM((2 * RANK, TOK), BF16),
            pltpu.VMEM((2 * RANK, PAD), BF16),
            pltpu.VMEM((RANK, 2 * RANK), F32),
            pltpu.VMEM((PAD, RANK), F32),
            pltpu.VMEM((4, 8, RANK), F32),
            pltpu.VMEM((16, 8, RANK), F32),
            pltpu.VMEM((2, 8, RANK), F32),
            pltpu.VMEM((OWNED, 1, TILE), F32),
            *sums,
            *sums,
            pltpu.SemaphoreType.DMA((6,)),
            pltpu.SemaphoreType.DMA((2 * N_MSG,)),
            pltpu.SemaphoreType.DMA((2 * N_MSG,)),
            pltpu.SemaphoreType.DMA((19,)),
            pltpu.SemaphoreType.DMA((19,)),
        ],
        compiler_params=pltpu.CompilerParams(
            collective_id=0, has_side_effects=True, vmem_limit_bytes=42 * 1024 * 1024
        ),
        name="compress",
    )(at, gt, error, q, momentum)


def finish(merged, oo, qq, qn, own, norm, momentum):
    rows = TILE // 4

    def block(m_ref, o_ref, q_ref, n_ref, own_ref, norm_ref, mom_ref, out_ref, next_ref, qn_ref):
        i = pl.program_id(0)
        at = pl.ds(pl.multiple_of(i * rows, 16), rows)
        columns = [pl.ds(n * PIECE, min(PIECE, TILE - n * PIECE)) for n in range(8)]
        for k in columns:
            out_ref[:, k] = (m_ref[at, k] - mm_t(o_ref[at, :], q_ref[k, :])).astype(BF16)
        qn_ref[...] = n_ref[at, :]

        @pl.when(i == 0)
        def _():
            rms = jnp.sqrt(norm_ref[:1, :1] / (D * D))
            scale = 0.1 / (rms + 1e-6)
            for k in columns:
                next_ref[:, 0, k] = 0.9 * mom_ref[:, k] + scale * mm_t(own_ref[...], q_ref[k, :])[:OWNED]

    vmem = pl.BlockSpec(memory_space=pltpu.VMEM)
    held = [pltpu.with_memory_space_constraint(v, pltpu.VMEM) for v in (merged, oo, qq, qn, own, norm, momentum)]
    whole = pl.BlockSpec((OWNED, 1, TILE), lambda i: (0, 0, 0))
    return pl.pallas_call(
        block,
        grid=(4,),
        out_shape=(
            jax.ShapeDtypeStruct((TILE, TILE), BF16),
            jax.ShapeDtypeStruct((OWNED, 1, TILE), F32),
            jax.ShapeDtypeStruct((TILE, RANK), F32),
        ),
        in_specs=[vmem] * 7,
        out_specs=(
            pl.BlockSpec((rows, TILE), lambda i: (i, 0)),
            whole,
            pl.BlockSpec((rows, RANK), lambda i: (i, 0)),
        ),
        compiler_params=pltpu.CompilerParams(vmem_limit_bytes=16 * 1024 * 1024),
        name="finish",
    )(*held)


def per_device(acts, grads, error, momentum, q_start):
    at, gt = acts[:, 0, :].T, grads[:, 0, :].T
    made = compress(at, gt, error[0, 0], q_start[0], jnp.swapaxes(momentum, 0, 1))
    error_next, momentum_next, q_tile = finish(*made)
    return (error_next[None, None], jnp.swapaxes(momentum_next, 0, 1), q_tile[None])


def solution(mesh):
    split_mesh = Mesh(mesh.devices.reshape(4, 4, 2, mesh.shape["mp"]), (*DP, "mp"))
    in_specs = (
        P(DP, "mp", None),
        P(DP, "mp", None),
        P(DP, "mp", None, None),
        P("mp", DP, None),
        P("mp", None, None),
    )
    out_specs = (P(DP, "mp", None, None), P("mp", DP, None), P("mp", None, None))
    return jax.shard_map(
        per_device, mesh=split_mesh, in_specs=in_specs, out_specs=out_specs, check_vma=False
    )
```
